32 devices in a mesh: tm: 16 (over z, y, x), tile: 2 (over core).
Axes of the slice: x: 2, y: 2, z: 4, core: 2. Of those that a mesh axis runs over, the one named last changes fastest.
Arguments:
- prior_space: float32 [1536, 1536], P('tile'), as said below
- node_gain: float32 [1536], replicated, may hold values from 0.4 to 1
- time_diag: float32 [32], P('tm'), may hold values from 0.6 to 1.5
- rho: float32 [32], P('tm'), may hold values from 0.2 to 0.95
- obs_values: float32 [2, 512, 16, 768], P('tile', 'tm'), may hold values from -1 to 1
- obs_weight: float32 [2, 512, 16], P('tile', 'tm'), may hold values from 0.25 to 4
- obs_step: int32 [2, 16, 32], P('tile', 'tm'), may hold values from 0 to 31, each once within a row
Outputs:
- separator_block: float32 [16, 1536, 1536], P('tm', 'tile')
- separator_coupling: float32 [16, 1536, 1536], P('tm', 'tile')
- interior_logdet: float32 [16], P('tm')
The draws below stay inside these ranges and needn't reach their ends.
Inputs may be any that keep to these rules, and one draw needn't show every extreme that they name: prior_space is symmetric and each diagonal entry exceeds the sum of magnitudes of the other entries of its row. For each node block c and each index m of tm, obs_step[c, m] names every time step exactly once.
All inputs are finite; a program needn't handle non-finite values.
Results may differ from the reference program's by a relative error of at most 0.00013.
Values sent between devices are 32-bit elements; how exact they have to be, the bound alone decides.
A program may use at most 192 MiB of HBM per device.

```python
import math
import jax
import jax.numpy as jnp
from jax import lax

NODES = 1536
OBS_BLK = 16
BLOCK = 768
STEPS = 32
OBS_DEV = 32
N_TM = 16
N_TILE = 2


def draw_prior_space(key, part):
    key_mod, key_diag = jax.random.split(key, 2)
    strength = 4.0
    reach = NODES / 64.0
    bound_total = 2.0 / (math.exp(1.0 / reach) - 1.0)
    order = jnp.arange(NODES, dtype=jnp.float32)
    modulate = jax.random.uniform(key_mod, (NODES, NODES), jnp.float32, 0.8, 1.0)
    symmetric = 0.5 * (modulate + modulate.T)
    distance = jnp.abs(order[:, None] - order[None, :])
    off_part = -(strength / bound_total) * jnp.exp(-distance / reach) * symmetric
    diag_vals = strength * jax.random.uniform(key_diag, (NODES,), jnp.float32, 1.02, 1.25)
    row_ids = lax.broadcasted_iota(jnp.int32, (NODES, NODES), 0)
    col_ids = lax.broadcasted_iota(jnp.int32, (NODES, NODES), 1)
    return jnp.where(row_ids == col_ids, diag_vals[:, None] * jnp.ones((1, NODES), jnp.float32), off_part)


def level_of(key, dims, cuts, least, top_value):
    level, own = 1.0, jax.random.fold_in(key, 6)
    for axis_at, blocks in cuts:
        draws = jnp.exp(jax.random.uniform(jax.random.fold_in(own, axis_at), (blocks,), jnp.float32, least / len(cuts), top_value / len(cuts)))
        level = level * jnp.repeat(draws, dims[axis_at] // blocks).reshape([-1 if axis == axis_at else 1 for axis in range(len(dims))])
    return level


def centred(stream_key, extent, width, limit, shards=(), kind=jnp.bfloat16):
    array = width * jax.random.normal(stream_key, extent, jnp.float32)
    if shards:
        array = array * level_of(stream_key, extent, shards, -0.22, 0.18)
    return jnp.clip(array, -limit, limit).astype(kind)


def setup_inputs(seed: int = 0) -> dict:
    key_list = jax.random.split(jax.random.key(seed), 8)
    prior_space = draw_prior_space(jax.random.fold_in(key_list[7], 71), 0)
    node_gain = jnp.clip(jax.random.uniform(key_list[1], (NODES,), jnp.float32, 0.4, 1.0), 0.4, 1.0)
    time_diag = jnp.clip(jnp.exp(math.log(1.5) - 0.9162907 * jax.random.uniform(key_list[2], (STEPS,), jnp.float32) ** level_of(key_list[2], (STEPS,), ((0, 16),), -0.2, 0.2)), 0.6, 1.5)
    rho = jnp.clip(0.2 + 0.75 * jax.random.uniform(key_list[3], (STEPS,), jnp.float32) ** level_of(key_list[3], (STEPS,), ((0, 16),), -0.2, 0.2), 0.2, 0.95)
    obs_values = centred(key_list[4], (N_TILE, N_TM * OBS_DEV, OBS_BLK, BLOCK), (1.0 / (N_TM * OBS_BLK) ** 0.5), 1.0, ((0, 2), (1, 16)), jnp.float32)
    obs_weight = jnp.clip(jnp.exp(math.log(4.0) - 2.7725887 * jax.random.uniform(key_list[5], (N_TILE, N_TM * OBS_DEV, OBS_BLK), jnp.float32) ** level_of(key_list[5], (N_TILE, N_TM * OBS_DEV, OBS_BLK), ((0, 2), (1, 16)), -0.2, 0.2)), 0.25, 4.0)
    obs_step = jax.vmap(lambda own: jax.random.permutation(own, STEPS))(jax.random.split(key_list[6], N_TILE * N_TM)).reshape((N_TILE, N_TM, STEPS)).astype(jnp.int32)
    return {"prior_space": prior_space, "node_gain": node_gain, "time_diag": time_diag, "rho": rho, "obs_values": obs_values, "obs_weight": obs_weight, "obs_step": obs_step}


def reference(prior_space, node_gain, time_diag, rho, obs_values, obs_weight, obs_step):
    precise = lax.Precision.HIGHEST
    scaled = obs_values * obs_weight[..., None]
    tile_steps = obs_step.reshape(N_TILE, N_TM * OBS_DEV)

    def add_tile(grams, inputs):
        scaled_tile, plain_tile, step_ids = inputs
        terms = jnp.einsum('crb,crd->cbd', scaled_tile, plain_tile, precision=precise)

        def place(gram_block, step_id, term_block):
            current = lax.dynamic_index_in_dim(gram_block, step_id, 0, keepdims=False)
            return lax.dynamic_update_index_in_dim(gram_block, current + term_block, step_id, 0)
        return (jax.vmap(place)(grams, step_ids, terms), None)
    start_grams = jnp.zeros((N_TILE, STEPS, BLOCK, BLOCK), jnp.float32)
    grams, unused = lax.scan(add_tile, start_grams, (jnp.swapaxes(scaled, 0, 1), jnp.swapaxes(obs_values, 0, 1), jnp.swapaxes(tile_steps, 0, 1)))
    grams = jnp.transpose(grams.reshape(N_TILE, N_TM, 2, BLOCK, BLOCK), (1, 2, 0, 3, 4))
    picker = jnp.eye(N_TILE, dtype=jnp.float32)

    def assemble(coef, gram_step):
        placed = gram_step[:, :, None, :] * picker[:, None, :, None]
        return coef * prior_space + placed.reshape(NODES, NODES)
    coefs = time_diag.reshape(N_TM, 2)
    rates = rho.reshape(N_TM, 2)
    gain_matrix = jnp.diag(node_gain)

    def interior(inputs):
        coef, gram_step = inputs
        matrix = assemble(coef, gram_step)
        lower_factor = jnp.linalg.cholesky(matrix)
        log_det = 2.0 * jnp.sum(jnp.log(jnp.diagonal(lower_factor))) / NODES
        half_solve = lax.linalg.triangular_solve(lower_factor, gain_matrix, left_side=True, lower=True)
        inverse_cols = lax.linalg.triangular_solve(lower_factor, half_solve, left_side=True, lower=True, transpose_a=True)
        return (node_gain[:, None] * inverse_cols, log_det)
    schur_all, interior_logdet = lax.map(interior, (coefs[:, 0], grams[:, 0]))
    shifted = rates[1:, 0][:, None, None] ** 2 * schur_all[1:]
    following = jnp.concatenate([shifted, jnp.zeros((1, NODES, NODES), jnp.float32)], axis=0)
    separators = lax.map(lambda inputs: assemble(inputs[0], inputs[1]), (coefs[:, 1], grams[:, 1]))
    separator_block = separators - rates[:, 1][:, None, None] ** 2 * schur_all - following
    separator_coupling = -(rates[:, 0] * rates[:, 1])[:, None, None] * schur_all
    return (separator_block, separator_coupling, interior_logdet)
```

```python
import functools
import jax, jax.numpy as jnp
from jax import lax
from jax.experimental import pallas as pl
from jax.experimental.pallas import tpu as pltpu
from jax.sharding import PartitionSpec as P

REG = (8, 128)
BIG, SMALL = 256, 64


def along(x, j):
    return jnp.broadcast_to(x[:, j:j + 1], REG)


def down(x, i):
    return jnp.take_along_axis(x, jnp.full(REG, i, jnp.int32), axis=0)


def halves(x):
    high = x.astype(jnp.bfloat16)
    return high, (x - high.astype(jnp.float32)).astype(jnp.bfloat16)


def dot_nn(a, b):
    ah, al = halves(a)
    bh, bl = halves(b)
    return jnp.dot(jnp.concatenate([ah, al, ah], 1), jnp.concatenate([bh, bh, bl], 0), preferred_element_type=jnp.float32)


def pair_inverse(a, b, d):
    det = a * d - b * b
    r = 1.0 / det
    return d * r, -(b * r), a * r, det


def inverse_of_four(s):
    a, b, d, det1 = pair_inverse(s[0, 0], s[1, 0], s[1, 1])
    q = [[s[2, 0], s[2, 1]], [s[3, 0], s[3, 1]]]
    m = [[q[i][0] * a + q[i][1] * b, q[i][0] * b + q[i][1] * d] for i in range(2)]
    u = s[2, 2] - (m[0][0] * q[0][0] + m[0][1] * q[0][1])
    v = s[3, 2] - (m[1][0] * q[0][0] + m[1][1] * q[0][1])
    w = s[3, 3] - (m[1][0] * q[1][0] + m[1][1] * q[1][1])
    u, v, w, det2 = pair_inverse(u, v, w)
    low = [[u * m[0][j] + v * m[1][j] for j in range(2)], [v * m[0][j] + w * m[1][j] for j in range(2)]]
    w00 = a + (m[0][0] * low[0][0] + m[1][0] * low[1][0])
    w01 = b + (m[0][0] * low[0][1] + m[1][0] * low[1][1])
    w11 = d + (m[0][1] * low[0][1] + m[1][1] * low[1][1])
    inverse = [[w00, w01, -low[0][0], -low[1][0]],
               [w01, w11, -low[0][1], -low[1][1]],
               [-low[0][0], -low[0][1], u, v],
               [-low[1][0], -low[1][1], v, w]]
    return inverse, det1, det2


def eliminate(tiles, log_det, offset):
    lane = lax.broadcasted_iota(jnp.int32, REG, 1) - offset
    sub = lax.broadcasted_iota(jnp.int32, REG, 0)
    for p in range(0, 8 * len(tiles), 4):
        home, first = p // 8, p % 8
        cols = [[along(t, offset + p + j) for t in tiles] for j in range(4)]
        s = {(i, j): down(cols[j][home], first + i) for j in range(4) for i in range(j, 4)}
        inv, det1, det2 = inverse_of_four(s)
        log_det = log_det + (jnp.log(det1) + jnp.log(det2))
        here = (lane >= p) & (lane < p + 4)
        rows = [jnp.where(here, jnp.where(lane == p + i, 1.0, 0.0), down(tiles[home], first + i)) for i in range(4)]
        out = [(inv[i][0] * rows[0] + inv[i][1] * rows[1]) + (inv[i][2] * rows[2] + inv[i][3] * rows[3]) for i in range(4)]
        new = []
        for t, tile in enumerate(tiles):
            kept = jnp.where(here, 0.0, tile)
            kept = kept - ((cols[0][t] * out[0] + cols[1][t] * out[1]) + (cols[2][t] * out[2] + cols[3][t] * out[3]))
            if t == home:
                for i in range(4):
                    kept = jnp.where(sub == first + i, out[i], kept)
            new.append(kept)
        tiles = new
    return tiles, log_det


def small_step(s, d_ref, ld_ref):
    half, offset = s // 2, (s % 2) * SMALL
    mine, others = slice(128 * half, 128 * half + 128), slice(128 * (1 - half), 128 * (1 - half) + 128)
    at = slice(SMALL * s, SMALL * s + SMALL)
    tiles = [d_ref[SMALL * s + 8 * t:SMALL * s + 8 * t + 8, mine] for t in range(SMALL // 8)]
    tiles, ld = eliminate(tiles, ld_ref[...], offset)
    ld_ref[...] = ld
    panel = jnp.concatenate(tiles, 0)
    lane = lax.broadcasted_iota(jnp.int32, (SMALL, 128), 1)
    pivot = (lane >= offset) & (lane < offset + SMALL)
    gap = jnp.zeros((SMALL, 128), jnp.float32)

    def padded(x):
        return jnp.concatenate([x, gap] if offset == 0 else [gap, x], 0)

    across = dot_nn(jnp.where(pivot, panel, 0.0), padded(d_ref[at, others]))
    row = [panel, across] if half == 0 else [across, panel]
    lane = lax.broadcasted_iota(jnp.int32, (BIG, 128), 1)
    pivot = (lane >= offset) & (lane < offset + SMALL)
    own = d_ref[:, mine]
    col = jnp.where(pivot, own, 0.0)
    d_ref[:, mine] = jnp.where(pivot, 0.0, own) - dot_nn(col, padded(panel))
    d_ref[:, others] -= dot_nn(col, padded(across))
    d_ref[at, :] = jnp.concatenate(row, 1)


def dot_nt(a, b):
    k = a.shape[1] // 2
    left = jnp.concatenate([a, a[:, :k]], 1)
    right = jnp.concatenate([b[:, :k], b[:, :k], b[:, k:]], 1)
    return lax.dot_general(left, right, (((1,), (1,)), ((), ())), preferred_element_type=jnp.float32)


def rows_of(i):
    return pl.ds(pl.multiple_of(i * BIG, BIG), BIG)


def split_to(ref, at, x):
    high, low = halves(x)
    ref[at, :BIG] = high
    ref[at, BIG:] = low


def make_units(k, count, x_ref, c_ref, g_ref, w_ref, ahead):
    others = [lax.rem(k + 1 + i, count) for i in range(count - 1)]

    def gain(i):
        def run():
            g = dot_nt(c_ref[rows_of(i), :], w_ref[...])
            split_to(g_ref, rows_of(i), g)
            x_ref[rows_of(i), rows_of(k)] = g
        return run

    def turned(j):
        def run():
            x_ref[rows_of(k), rows_of(j)] = dot_nt(w_ref[...], c_ref[rows_of(j), :])
        return run

    def update(u, v):
        def run():
            low, high = jnp.minimum(u, v), jnp.maximum(u, v)
            swept = low < k
            r, c = jnp.where(swept, low, high), jnp.where(swept, high, low)
            x_ref[rows_of(r), rows_of(c)] -= dot_nt(g_ref[rows_of(r), :], c_ref[rows_of(c), :])
        return run

    gains = [gain(i) for i in others[ahead:]]
    if not ahead:
        return gains + [turned(j) for j in others], [update(others[a], others[b]) for a in range(count - 1) for b in range(a, count - 1)]
    pairs = [(a, b) for a in range(count - 1) for b in range(a, count - 1) if (a, b) != (0, 0)]
    return gains + [turned(j) for j in others], [update(others[a], others[b]) for a, b in pairs]


def boundary(k, x_ref, d_ref, c_ref, g_ref, w_ref, count, ahead):
    w = d_ref[...]
    split_to(w_ref, slice(None), w)
    if ahead:
        q = k + 1
        split_to(c_ref, rows_of(q), x_ref[rows_of(q), rows_of(k)])
        g = dot_nt(c_ref[rows_of(q), :], w_ref[...])
        split_to(g_ref, rows_of(q), g)
        d_ref[...] = x_ref[rows_of(q), rows_of(q)] - dot_nt(g_ref[rows_of(q), :], c_ref[rows_of(q), :])
    for i in range(count):
        split_to(c_ref, slice(i * BIG, (i + 1) * BIG), x_ref[i * BIG:(i + 1) * BIG, rows_of(k)])
    x_ref[rows_of(k), rows_of(k)] = -w


def sweep_kernel(a_ref, x_ref, ld_ref, d_ref, c_ref, g_ref, w_ref):
    x_ref[...] = a_ref[...]
    count = x_ref.shape[0] // BIG
    ld_ref[...] = jnp.zeros_like(ld_ref)
    d_ref[...] = x_ref[:BIG, :BIG]
    for s in range(BIG // SMALL):
        small_step(s, d_ref, ld_ref)
    boundary(0, x_ref, d_ref, c_ref, g_ref, w_ref, count, True)

    def body(q, _):
        k = q - 1
        first, rest = make_units(k, count, x_ref, c_ref, g_ref, w_ref, 1)
        share = -(-len(rest) // 3)
        lists = [first] + [rest[i * share:(i + 1) * share] for i in range(3)]
        for s in range(BIG // SMALL):
            small_step(s, d_ref, ld_ref)
            for unit in lists[s]:
                unit()

        @pl.when(q < count - 1)
        def _():
            boundary(q, x_ref, d_ref, c_ref, g_ref, w_ref, count, True)
        return 0

    lax.fori_loop(1, count, body, 0)
    boundary(count - 1, x_ref, d_ref, c_ref, g_ref, w_ref, count, False)
    first, rest = make_units(count - 1, count, x_ref, c_ref, g_ref, w_ref, 0)
    for unit in first + rest:
        unit()


def sweep(a):
    n = a.shape[0]
    return pl.pallas_call(
        sweep_kernel,
        out_shape=(jax.ShapeDtypeStruct((n, n), jnp.float32), jax.ShapeDtypeStruct(REG, jnp.float32)),
        in_specs=[pl.BlockSpec(memory_space=pltpu.VMEM)],
        out_specs=(pl.BlockSpec(memory_space=pltpu.VMEM),) * 2,
        scratch_shapes=[
            pltpu.VMEM((BIG, BIG), jnp.float32),
            pltpu.VMEM((n, 2 * BIG), jnp.bfloat16),
            pltpu.VMEM((n, 2 * BIG), jnp.bfloat16),
            pltpu.VMEM((BIG, 2 * BIG), jnp.bfloat16),
        ],
        compiler_params=pltpu.CompilerParams(vmem_limit_bytes=40 << 20),
    )(a)


def order_kernel(step_ref, value_ref, weight_ref, out_ref):
    for k in range(value_ref.shape[0]):
        out_ref[step_ref[k]] = value_ref[k] * jnp.sqrt(weight_ref[k])


def by_step(values, weights, steps):
    return pl.pallas_call(
        order_kernel,
        out_shape=jax.ShapeDtypeStruct(values.shape, jnp.float32),
        in_specs=[
            pl.BlockSpec(memory_space=pltpu.SMEM),
            pl.BlockSpec(memory_space=pltpu.VMEM),
            pl.BlockSpec(memory_space=pltpu.VMEM),
        ],
        out_specs=pl.BlockSpec(memory_space=pltpu.VMEM),
        compiler_params=pltpu.CompilerParams(vmem_limit_bytes=40 << 20),
    )(steps, values, weights[..., None])


def gram(rows):
    return lax.dot_general(rows, rows, (((0,), (0,)), ((), ())), precision=lax.Precision.HIGH)


def mirrored(upper):
    block = jnp.arange(upper.shape[0]) // BIG
    return jnp.where(block[:, None] <= block[None, :], upper, upper.T)


def on_device(prior_space, node_gain, time_diag, rho, obs_values, obs_weight, obs_step):
    size, node_count = prior_space.shape
    parts = lax.axis_size("tm")
    first = lax.axis_index("tile") == 0
    last = lax.axis_index("tm") == parts - 1
    swap = [(0, 1), (1, 0)]

    def chosen(a, b):
        return jnp.where(first, a, b)

    sent = by_step(obs_values[0], obs_weight[0], obs_step[0, 0])
    sent = sent.reshape(parts, 2, sent.shape[1], size)
    even, odd = sent[:, 0], sent[:, 1]
    both = jnp.stack([even, jnp.roll(even, -1, 0)], 1).reshape(2 * parts, -1, size)
    both = lax.all_to_all(both, ("tm", "tile"), split_axis=0, concat_axis=0, tiled=True)
    both = both.reshape(parts, 2, -1, size)
    rows = [both[:, c].reshape(-1, size) for c in range(2)]
    odd = lax.all_to_all(odd, "tm", split_axis=0, concat_axis=0, tiled=True).reshape(-1, size)

    scalars = jnp.stack([time_diag[0], rho[0]])
    next_scalars = lax.ppermute(scalars, "tm", [(i + 1, i) for i in range(parts - 1)])
    weight = chosen(time_diag[0], jnp.where(last, 1.0, next_scalars[0]))

    prior_own = chosen(prior_space[:, :size], prior_space[:, size:])
    prior_cross = chosen(prior_space[:, size:], prior_space[:, :size])
    prior_swapped = lax.ppermute(prior_own, "tile", swap)
    gain_own = chosen(node_gain[:size], node_gain[size:])
    gain_other = chosen(node_gain[size:], node_gain[:size])
    block_other = weight * prior_swapped + gram(chosen(rows[1], rows[0]))
    block_own = weight * prior_own + gram(chosen(rows[0], rows[1]))

    def scale_of(a):
        return lax.rsqrt(jnp.sum(jnp.where(jnp.eye(size, dtype=jnp.bool_), a, 0.0), 1))

    scale_other, scale_own = scale_of(block_other), scale_of(block_own)
    scale = jnp.concatenate([scale_other, scale_own])
    whole = jnp.concatenate([
        jnp.concatenate([block_other, jnp.zeros((size, size), jnp.float32)], 1),
        jnp.concatenate([weight * prior_cross, block_own], 1)], 0)
    swept, log_det = sweep(whole * scale[:, None] * scale[None, :])
    log_det = log_det[0, 0] - 2.0 * jnp.sum(jnp.log(scale))
    log_first = lax.ppermute(log_det.reshape(1), "tile", [(0, 1)])
    interior_logdet = chosen(log_det.reshape(1), log_first) / node_count

    left_other, left_own = scale_other * gain_other, scale_own * gain_own
    upper = -swept[:size, :size] * left_other[:, None] * left_other[None, :]
    corner = -swept[:size, size:] * left_other[:, None] * left_own[None, :]
    lower = -swept[size:, size:] * left_own[:, None] * left_own[None, :]
    got_own = mirrored(lax.ppermute(upper, "tile", swap))
    got_cross = lax.ppermute(corner, "tile", swap)
    have_own = mirrored(lower)
    have_cross = corner.T

    now_own, now_cross = chosen(have_own, got_own), chosen(have_cross, got_cross)
    next_own, next_cross = chosen(got_own, have_own), chosen(got_cross, have_cross)

    def in_order(own, cross):
        return chosen(jnp.concatenate([own, cross], 1), jnp.concatenate([cross, own], 1))

    now, following = in_order(now_own, now_cross), in_order(next_own, next_cross)
    separator = time_diag[1] * prior_space + in_order(gram(odd), jnp.zeros((size, size), jnp.float32))
    rate = next_scalars[1] * next_scalars[1]
    separator_block = separator - rho[1] * rho[1] * now - rate * following
    separator_coupling = -(rho[0] * rho[1]) * now
    return separator_block[None], separator_coupling[None], interior_logdet


def solution(mesh):
    in_specs = (
        P("tile", None),
        P(),
        P("tm"),
        P("tm"),
        P("tile", "tm", None, None),
        P("tile", "tm", None),
        P("tile", "tm", None),
    )
    out_specs = (P("tm", "tile", None), P("tm", "tile", None), P("tm"))
    return jax.shard_map(
        on_device, mesh=mesh, in_specs=in_specs, out_specs=out_specs, check_vma=False
    )
```

```python
import functools
import jax, jax.numpy as jnp
from jax import lax
from jax.experimental import pallas as pl
from jax.experimental.pallas import tpu as pltpu
from jax.sharding import PartitionSpec as P

REG = (8, 128)
BIG, SMALL = 256, 64


def along(x, j):
    return jnp.broadcast_to(x[:, j:j + 1], REG)


def down(x, i):
    return jnp.take_along_axis(x, jnp.full(REG, i, jnp.int32), axis=0)


def halves(x):
    high = x.astype(jnp.bfloat16)
    return high, (x - high.astype(jnp.float32)).astype(jnp.bfloat16)


def dot_nn(a, b):
    ah, al = halves(a)
    bh, bl = halves(b)
    return jnp.dot(jnp.concatenate([ah, al, ah], 1), jnp.concatenate([bh, bh, bl], 0), preferred_element_type=jnp.float32)


def pair_inverse(a, b, d):
    det = a * d - b * b
    r = 1.0 / det
    return d * r, -(b * r), a * r, det


def inverse_of_four(s):
    a, b, d, det1 = pair_inverse(s[0, 0], s[1, 0], s[1, 1])
    q = [[s[2, 0], s[2, 1]], [s[3, 0], s[3, 1]]]
    m = [[q[i][0] * a + q[i][1] * b, q[i][0] * b + q[i][1] * d] for i in range(2)]
    u = s[2, 2] - (m[0][0] * q[0][0] + m[0][1] * q[0][1])
    v = s[3, 2] - (m[1][0] * q[0][0] + m[1][1] * q[0][1])
    w = s[3, 3] - (m[1][0] * q[1][0] + m[1][1] * q[1][1])
    u, v, w, det2 = pair_inverse(u, v, w)
    low = [[u * m[0][j] + v * m[1][j] for j in range(2)], [v * m[0][j] + w * m[1][j] for j in range(2)]]
    w00 = a + (m[0][0] * low[0][0] + m[1][0] * low[1][0])
    w01 = b + (m[0][0] * low[0][1] + m[1][0] * low[1][1])
    w11 = d + (m[0][1] * low[0][1] + m[1][1] * low[1][1])
    inverse = [[w00, w01, -low[0][0], -low[1][0]],
               [w01, w11, -low[0][1], -low[1][1]],
               [-low[0][0], -low[0][1], u, v],
               [-low[1][0], -low[1][1], v, w]]
    return inverse, det1, det2


def eliminate(tiles, log_det, offset):
    lane = lax.broadcasted_iota(jnp.int32, REG, 1) - offset
    sub = lax.broadcasted_iota(jnp.int32, REG, 0)
    for p in range(0, 8 * len(tiles), 4):
        home, first = p // 8, p % 8
        cols = [[along(t, offset + p + j) for t in tiles] for j in range(4)]
        s = {(i, j): down(cols[j][home], first + i) for j in range(4) for i in range(j, 4)}
        inv, det1, det2 = inverse_of_four(s)
        log_det = log_det + (jnp.log(det1) + jnp.log(det2))
        here = (lane >= p) & (lane < p + 4)
        rows = [jnp.where(here, jnp.where(lane == p + i, 1.0, 0.0), down(tiles[home], first + i)) for i in range(4)]
        out = [(inv[i][0] * rows[0] + inv[i][1] * rows[1]) + (inv[i][2] * rows[2] + inv[i][3] * rows[3]) for i in range(4)]
        new = []
        for t, tile in enumerate(tiles):
            kept = jnp.where(here, 0.0, tile)
            kept = kept - ((cols[0][t] * out[0] + cols[1][t] * out[1]) + (cols[2][t] * out[2] + cols[3][t] * out[3]))
            if t == home:
                for i in range(4):
                    kept = jnp.where(sub == first + i, out[i], kept)
            new.append(kept)
        tiles = new
    return tiles, log_det


def small_step(s, d_ref, ld_ref):
    half, offset = s // 2, (s % 2) * SMALL
    mine, others = slice(128 * half, 128 * half + 128), slice(128 * (1 - half), 128 * (1 - half) + 128)
    at = slice(SMALL * s, SMALL * s + SMALL)
    tiles = [d_ref[SMALL * s + 8 * t:SMALL * s + 8 * t + 8, mine] for t in range(SMALL // 8)]
    tiles, ld = eliminate(tiles, ld_ref[...], offset)
    ld_ref[...] = ld
    panel = jnp.concatenate(tiles, 0)
    lane = lax.broadcasted_iota(jnp.int32, (SMALL, 128), 1)
    pivot = (lane >= offset) & (lane < offset + SMALL)
    gap = jnp.zeros((SMALL, 128), jnp.float32)

    def padded(x):
        return jnp.concatenate([x, gap] if offset == 0 else [gap, x], 0)

    across = dot_nn(jnp.where(pivot, panel, 0.0), padded(d_ref[at, others]))
    row = [panel, across] if half == 0 else [across, panel]
    lane = lax.broadcasted_iota(jnp.int32, (BIG, 128), 1)
    pivot = (lane >= offset) & (lane < offset + SMALL)
    own = d_ref[:, mine]
    col = jnp.where(pivot, own, 0.0)
    d_ref[:, mine] = jnp.where(pivot, 0.0, own) - dot_nn(col, padded(panel))
    d_ref[:, others] -= dot_nn(col, padded(across))
    d_ref[at, :] = jnp.concatenate(row, 1)


def dot_nt(a, b):
    k = a.shape[1] // 2
    left = jnp.concatenate([a, a[:, :k]], 1)
    right = jnp.concatenate([b[:, :k], b[:, :k], b[:, k:]], 1)
    return lax.dot_general(left, right, (((1,), (1,)), ((), ())), preferred_element_type=jnp.float32)


def rows_of(i):
    return pl.ds(pl.multiple_of(i * BIG, BIG), BIG)


def split_to(ref, at, x):
    high, low = halves(x)
    ref[at, :BIG] = high
    ref[at, BIG:] = low


def others_of(k, count):
    return [lax.rem(k + 1 + i, count) for i in range(count - 1)]


def gain(i, k, x_ref, c_ref, g_ref, w_ref):
    g = dot_nt(c_ref[rows_of(i), :], w_ref[...])
    split_to(g_ref, rows_of(i), g)
    x_ref[rows_of(i), rows_of(k)] = g


def update(u, v, k, x_ref, c_ref, g_ref):
    low, high = jnp.minimum(u, v), jnp.maximum(u, v)
    r, c = jnp.where(low < k, low, high), jnp.where(low < k, high, low)
    x_ref[rows_of(r), rows_of(c)] -= dot_nt(g_ref[rows_of(r), :], c_ref[rows_of(c), :])


def background(k, count, x_ref, c_ref, g_ref, w_ref):
    others = others_of(k, count)

    def turned(j):
        x_ref[rows_of(k), rows_of(j)] = dot_nt(w_ref[...], c_ref[rows_of(j), :])

    first = [functools.partial(gain, i, k, x_ref, c_ref, g_ref, w_ref) for i in others[1:]]
    first += [functools.partial(turned, j) for j in others]
    pairs = [(a, b) for a in range(count - 1) for b in range(a, count - 1) if b > 0]
    rest = [functools.partial(update, others[a], others[b], k, x_ref, c_ref, g_ref) for a, b in pairs]
    share = -(-len(rest) // 3)
    return [first] + [rest[i * share:(i + 1) * share] for i in range(3)]


def boundary(k, x_ref, d_ref, c_ref, g_ref, w_ref, ahead):
    count = x_ref.shape[0] // BIG
    w = d_ref[...]
    split_to(w_ref, slice(None), w)
    if ahead:
        q = k + 1
        split_to(c_ref, rows_of(q), x_ref[rows_of(q), rows_of(k)])
        g = dot_nt(c_ref[rows_of(q), :], w_ref[...])
        split_to(g_ref, rows_of(q), g)
        d_ref[...] = x_ref[rows_of(q), rows_of(q)] - dot_nt(g_ref[rows_of(q), :], c_ref[rows_of(q), :])
    for i in range(count):
        split_to(c_ref, slice(i * BIG, (i + 1) * BIG), x_ref[i * BIG:(i + 1) * BIG, rows_of(k)])
    x_ref[rows_of(k), rows_of(k)] = -w


def eliminate_blocks(start, stop, x_ref, ld_ref, d_ref, c_ref, g_ref, w_ref):
    count = x_ref.shape[0] // BIG

    def body(q, _):
        work = background(q - 1, count, x_ref, c_ref, g_ref, w_ref)
        for s in range(BIG // SMALL):
            small_step(s, d_ref, ld_ref)
            for unit in work[s]:
                unit()

        @pl.when(q < stop - 1)
        def _():
            boundary(q, x_ref, d_ref, c_ref, g_ref, w_ref, True)
        return 0

    lax.fori_loop(start, stop, body, 0)


def turned_halves(ref, u):
    split_at = u.shape[0]
    high, low = halves(u.T)
    ref[:, :split_at] = high
    ref[:, split_at:] = low


def blocks_of(size):
    return [slice(i, i + BIG) for i in range(0, size, BIG)]


def first_kernel(weight_ref, other_ref, cross_ref, own_ref, rows_ref, row_ref, col_ref,
                 x_ref, d_ref, ld_ref, c_ref, g_ref, w_ref, u_ref):
    size = other_ref.shape[0]
    n = x_ref.shape[0]
    weight = weight_ref[0]
    turned_halves(u_ref, rows_ref[...] * row_ref[:, :size])
    for i, at in enumerate(blocks_of(size)):
        down_scale = col_ref[at, :] * weight
        low = slice(size + at.start, size + at.stop)
        low_scale = col_ref[low, :] * weight
        for j, to in enumerate(blocks_of(size)):
            if j <= i:
                x_ref[at, to] = other_ref[at, to] * down_scale * row_ref[:, to] + dot_nt(u_ref[at, :], u_ref[to, :])
                far = slice(size + to.start, size + to.stop)
                x_ref[low, far] = own_ref[at, to] * low_scale * row_ref[:, far]
            x_ref[low, to] = cross_ref[at, to] * low_scale * row_ref[:, to]
    ld_ref[...] = jnp.zeros_like(ld_ref)
    d_ref[...] = x_ref[:BIG, :BIG]
    for s in range(BIG // SMALL):
        small_step(s, d_ref, ld_ref)
    boundary(0, x_ref, d_ref, c_ref, g_ref, w_ref, True)
    eliminate_blocks(1, size // BIG, x_ref, ld_ref, d_ref, c_ref, g_ref, w_ref)


def second_kernel(x_in_ref, d_in_ref, ld_in_ref, rows_ref, row_ref, left_row_ref, left_col_ref,
                  send_ref, own_ref, ld_ref, x_ref, d_ref, c_ref, g_ref, w_ref, u_ref):
    n = x_ref.shape[0]
    size = own_ref.shape[0]
    count = n // BIG
    half = size // BIG
    x_ref[...] = x_in_ref[...]
    d_ref[...] = d_in_ref[...]
    ld_ref[...] = ld_in_ref[...]
    turned_halves(u_ref, rows_ref[...] * row_ref[:, size:])
    for i, at in enumerate(blocks_of(size)):
        for j, to in enumerate(blocks_of(size)):
            if j <= i:
                x_ref[size + at.start:size + at.stop, size + to.start:size + to.stop] += dot_nt(u_ref[at, :], u_ref[to, :])
    boundary(half - 1, x_ref, d_ref, c_ref, g_ref, w_ref, True)
    eliminate_blocks(half, count, x_ref, ld_ref, d_ref, c_ref, g_ref, w_ref)
    k = count - 1
    w = d_ref[...]
    split_to(w_ref, slice(None), w)
    x_ref[k * BIG:n, k * BIG:n] = -w

    def finish(a, b, value):
        rows, cols = slice(a * BIG, a * BIG + BIG), slice(b * BIG, b * BIG + BIG)
        value = -value * left_col_ref[rows, :] * left_row_ref[:, cols]
        if a < half:
            send_ref[rows, cols] = value
        else:
            own_ref[(a - half) * BIG:(a - half) * BIG + BIG, (b - half) * BIG:(b - half) * BIG + BIG] = value

    finish(k, k, -w)
    for i in range(k):
        at = slice(i * BIG, i * BIG + BIG)
        c = x_ref[at, k * BIG:n]
        split_to(c_ref, at, c)
        g = dot_nt(c_ref[at, :], w_ref[...])
        split_to(g_ref, at, g)
        finish(i, k, g)
    for a in range(k):
        at = slice(a * BIG, a * BIG + BIG)
        for b in range(a, k):
            to = slice(b * BIG, b * BIG + BIG)
            finish(a, b, x_ref[at, to] - dot_nt(g_ref[at, :], c_ref[to, :]))


def states(n, rows):
    return [
        pltpu.VMEM((n, 2 * BIG), jnp.bfloat16),
        pltpu.VMEM((n, 2 * BIG), jnp.bfloat16),
        pltpu.VMEM((BIG, 2 * BIG), jnp.bfloat16),
        pltpu.VMEM((n // 2, 2 * rows), jnp.bfloat16),
    ]


def in_vmem(count):
    return [pl.BlockSpec(memory_space=pltpu.VMEM)] * count


def first_half(weight, other, cross, own, rows, scale):
    n = 2 * other.shape[0]
    f32 = jnp.float32
    return pl.pallas_call(
        first_kernel,
        out_shape=(jax.ShapeDtypeStruct((n, n), f32), jax.ShapeDtypeStruct((BIG, BIG), f32), jax.ShapeDtypeStruct(REG, f32)),
        in_specs=[pl.BlockSpec(memory_space=pltpu.SMEM)] + in_vmem(6),
        out_specs=tuple(in_vmem(3)),
        scratch_shapes=states(n, rows.shape[0]),
        compiler_params=pltpu.CompilerParams(vmem_limit_bytes=48 << 20),
        cost_estimate=pl.CostEstimate(flops=12 * n**3, bytes_accessed=8 * n * n, transcendentals=0),
    )(weight.reshape(1), other, cross, own, rows, scale[None, :], scale[:, None])


def second_half(x, d, log_det, rows, scale, left):
    n = x.shape[0]
    size = n // 2
    f32 = jnp.float32
    return pl.pallas_call(
        second_kernel,
        out_shape=(jax.ShapeDtypeStruct((size, n), f32), jax.ShapeDtypeStruct((size, size), f32), jax.ShapeDtypeStruct(REG, f32)),
        in_specs=in_vmem(7),
        out_specs=tuple(in_vmem(3)),
        scratch_shapes=[pltpu.VMEM((n, n), f32), pltpu.VMEM((BIG, BIG), f32)] + states(n, rows.shape[0]),
        compiler_params=pltpu.CompilerParams(vmem_limit_bytes=48 << 20),
        cost_estimate=pl.CostEstimate(flops=12 * n**3, bytes_accessed=8 * n * n, transcendentals=0),
    )(x, d, log_det, rows, scale[None, :], left[None, :], left[:, None])


def last_kernel(numbers_ref, first_ref, prior_ref, rows_ref, own_ref, sent_ref, got_ref,
                block_ref, coupling_ref, block_buf, coupling_buf, u_ref, sems):
    size, n = prior_ref.shape
    weight, have_block, got_block, have_coupling, got_coupling = [numbers_ref[i] for i in range(5)]
    own_at = first_ref[0] * size
    cross_at = size - own_at
    turned_halves(u_ref, rows_ref[...])
    copies = []
    for i, at in enumerate(blocks_of(size)):
        for j, to in enumerate(blocks_of(size)):
            for which in range(2):
                if which == 0:
                    have = own_ref[at, to] if i <= j else own_ref[to, at].T
                    got = got_ref[at, to] if i <= j else got_ref[to, at].T
                    cols = pl.ds(pl.multiple_of(own_at + j * BIG, BIG), BIG)
                else:
                    have = sent_ref[to, size + at.start:size + at.stop].T
                    got = got_ref[at, size + to.start:size + to.stop]
                    cols = pl.ds(pl.multiple_of(cross_at + j * BIG, BIG), BIG)
                base = weight * prior_ref[at, cols]
                if which == 0:
                    base = base + dot_nt(u_ref[at, :], u_ref[to, :])
                block_buf[at, cols] = base - (have_block * have + got_block * got)
                coupling_buf[at, cols] = have_coupling * have + got_coupling * got
        for o, (buf, ref) in enumerate([(block_buf, block_ref), (coupling_buf, coupling_ref)]):
            copy = pltpu.make_async_copy(buf.at[at], ref.at[at], sems.at[2 * i + o])
            copy.start()
            copies.append(copy)
    for copy in copies:
        copy.wait()


def outputs(numbers, tile, prior, rows, own, sent, got):
    size, n = prior.shape
    f32 = jnp.float32
    return pl.pallas_call(
        last_kernel,
        out_shape=(jax.ShapeDtypeStruct((size, n), f32),) * 2,
        in_specs=[pl.BlockSpec(memory_space=pltpu.SMEM)] * 2 + in_vmem(5),
        out_specs=(pl.BlockSpec(memory_space=pl.ANY),) * 2,
        scratch_shapes=[pltpu.VMEM((size, n), f32)] * 2
        + [pltpu.VMEM((size, 2 * rows.shape[0]), jnp.bfloat16), pltpu.SemaphoreType.DMA((2 * size // BIG,))],
        compiler_params=pltpu.CompilerParams(vmem_limit_bytes=48 << 20),
        cost_estimate=pl.CostEstimate(flops=6 * size * size * n, bytes_accessed=20 * size * n, transcendentals=0),
    )(numbers, tile, prior, rows, own, sent, got)


def order_kernel(step_ref, value_ref, weight_ref, out_ref):
    for k in range(value_ref.shape[0]):
        out_ref[step_ref[k]] = value_ref[k] * jnp.sqrt(weight_ref[k])


def by_step(values, weights, steps):
    return pl.pallas_call(
        order_kernel,
        out_shape=jax.ShapeDtypeStruct(values.shape, jnp.float32),
        in_specs=[
            pl.BlockSpec(memory_space=pltpu.SMEM),
            pl.BlockSpec(memory_space=pltpu.VMEM),
            pl.BlockSpec(memory_space=pltpu.VMEM),
        ],
        out_specs=pl.BlockSpec(memory_space=pltpu.VMEM),
        compiler_params=pltpu.CompilerParams(vmem_limit_bytes=40 << 20),
    )(steps, values, weights[..., None])


def spread(rows):
    return lax.all_to_all(rows, "tm", split_axis=0, concat_axis=0, tiled=True).reshape(-1, rows.shape[-1])


def on_device(prior_space, node_gain, time_diag, rho, obs_values, obs_weight, obs_step):
    size, node_count = prior_space.shape
    parts = lax.axis_size("tm")
    tile = lax.axis_index("tile")
    first = tile == 0
    last = lax.axis_index("tm") == parts - 1
    swap = [(0, 1), (1, 0)]

    def chosen(a, b):
        return jnp.where(first, a, b)

    sent = by_step(obs_values[0], obs_weight[0], obs_step[0, 0])
    sent = sent.reshape(parts, 2, sent.shape[1], size)
    even, odd = sent[:, 0], sent[:, 1]
    after = jnp.roll(even, -1, 0)
    for_other = lax.ppermute(chosen(after, even), "tile", swap)
    rows_other = spread(for_other)
    rest = jnp.concatenate([chosen(even, after), odd], 1)
    rest, rows_other = lax.optimization_barrier((rest, rows_other))
    rest = lax.all_to_all(rest, "tm", split_axis=0, concat_axis=0, tiled=True)
    rows_own, rows_odd = [rest[:, s * even.shape[1]:(s + 1) * even.shape[1]].reshape(-1, size) for s in range(2)]

    scalars = jnp.stack([time_diag[0], rho[0]])
    next_scalars = lax.ppermute(scalars, "tm", [(i + 1, i) for i in range(parts - 1)])
    weight = chosen(time_diag[0], jnp.where(last, 1.0, next_scalars[0]))

    prior_own = chosen(prior_space[:, :size], prior_space[:, size:])
    prior_cross = chosen(prior_space[:, size:], prior_space[:, :size])
    prior_other = lax.ppermute(prior_own, "tile", swap)
    gain_own = chosen(node_gain[:size], node_gain[size:])
    gain_other = chosen(node_gain[size:], node_gain[:size])
    here = jnp.eye(size, dtype=jnp.bool_)
    diagonal = jnp.concatenate([jnp.sum(jnp.where(here, p, 0.0), 1) for p in (prior_other, prior_own)])
    scale = lax.rsqrt(weight * diagonal)
    left = scale * jnp.concatenate([gain_other, gain_own])

    x, d, log_det = first_half(weight, prior_other, prior_cross, prior_own, rows_other, scale)
    send, own, log_det = second_half(x, d, log_det, rows_own, scale, left)
    log_det = log_det[0, 0] - 2.0 * jnp.sum(jnp.log(scale))
    log_first = lax.ppermute(log_det.reshape(1), "tile", [(0, 1)])
    interior_logdet = chosen(log_det.reshape(1), log_first) / node_count

    got = lax.ppermute(send, "tile", swap)
    now, following, across = rho[1] * rho[1], next_scalars[1] * next_scalars[1], -(rho[0] * rho[1])
    numbers = jnp.stack([time_diag[1], chosen(now, following), chosen(following, now), chosen(across, 0.0), chosen(0.0, across)])
    block, coupling = outputs(numbers, tile.reshape(1).astype(jnp.int32), prior_space, rows_odd, own, send, got)
    return block[None], coupling[None], interior_logdet


def solution(mesh):
    in_specs = (
        P("tile", None),
        P(),
        P("tm"),
        P("tm"),
        P("tile", "tm", None, None),
        P("tile", "tm", None),
        P("tile", "tm", None),
    )
    out_specs = (P("tm", "tile", None), P("tm", "tile", None), P("tm"))
    return jax.shard_map(
        on_device, mesh=mesh, in_specs=in_specs, out_specs=out_specs, check_vma=False
    )
```

```python
import functools
import jax, jax.numpy as jnp
from jax import lax
from jax.experimental import pallas as pl
from jax.experimental.pallas import tpu as pltpu
from jax.sharding import PartitionSpec as P

REG = (8, 128)
BIG, SMALL = 256, 64


def along(x, j):
    return jnp.broadcast_to(x[:, j:j + 1], REG)


def down(x, i):
    return jnp.take_along_axis(x, jnp.full(REG, i, jnp.int32), axis=0)


def halves(x):
    high = x.astype(jnp.bfloat16)
    return high, (x - high.astype(jnp.float32)).astype(jnp.bfloat16)


def dot_nn(a, b):
    ah, al = halves(a)
    bh, bl = halves(b)
    return jnp.dot(jnp.concatenate([ah, al, ah], 1), jnp.concatenate([bh, bh, bl], 0), preferred_element_type=jnp.float32)


def pair_inverse(a, b, d):
    det = a * d - b * b
    r = 1.0 / det
    return d * r, -(b * r), a * r, det


def inverse_of_four(s):
    a, b, d, det1 = pair_inverse(s[0, 0], s[1, 0], s[1, 1])
    q = [[s[2, 0], s[2, 1]], [s[3, 0], s[3, 1]]]
    m = [[q[i][0] * a + q[i][1] * b, q[i][0] * b + q[i][1] * d] for i in range(2)]
    u = s[2, 2] - (m[0][0] * q[0][0] + m[0][1] * q[0][1])
    v = s[3, 2] - (m[1][0] * q[0][0] + m[1][1] * q[0][1])
    w = s[3, 3] - (m[1][0] * q[1][0] + m[1][1] * q[1][1])
    u, v, w, det2 = pair_inverse(u, v, w)
    low = [[u * m[0][j] + v * m[1][j] for j in range(2)], [v * m[0][j] + w * m[1][j] for j in range(2)]]
    w00 = a + (m[0][0] * low[0][0] + m[1][0] * low[1][0])
    w01 = b + (m[0][0] * low[0][1] + m[1][0] * low[1][1])
    w11 = d + (m[0][1] * low[0][1] + m[1][1] * low[1][1])
    inverse = [[w00, w01, -low[0][0], -low[1][0]],
               [w01, w11, -low[0][1], -low[1][1]],
               [-low[0][0], -low[0][1], u, v],
               [-low[1][0], -low[1][1], v, w]]
    return inverse, det1, det2


def eliminate(tiles, log_det, offset):
    lane = lax.broadcasted_iota(jnp.int32, REG, 1) - offset
    sub = lax.broadcasted_iota(jnp.int32, REG, 0)
    for home in range(len(tiles)):
        p = 8 * home
        cols = [[along(t, offset + p + j) for t in tiles] for j in range(8)]
        c = [cols[j][home] for j in range(8)]
        head, det1, det2 = inverse_of_four({(i, j): down(c[j], i) for j in range(4) for i in range(j, 4)})
        slope = [weighted([head[i][j] for i in range(4)], c[:4]) for j in range(4)]
        rest = [c[j] - weighted([down(c[j], i) for i in range(4)], slope) for j in range(4, 8)]
        foot, det3, det4 = inverse_of_four({(i, j): down(rest[j], i + 4) for j in range(4) for i in range(j, 4)})
        log_det = log_det + ((jnp.log(det1) + jnp.log(det2)) + (jnp.log(det3) + jnp.log(det4)))
        here = (lane >= p) & (lane < p + 8)
        rows = jnp.where(here, jnp.where(lane == p + sub, 1.0, 0.0), tiles[home])
        top = [down(rows, i) for i in range(4)]
        upper = [weighted(head[i], top) for i in range(4)]
        rows = rows - weighted(c[:4], upper)
        low = [down(rows, i) for i in range(4, 8)]
        lower = [weighted(foot[i], low) for i in range(4)]
        upper = [upper[i] - weighted([down(slope[i], j) for j in range(4, 8)], lower) for i in range(4)]
        out = upper + lower
        new = []
        for t, tile in enumerate(tiles):
            if t == home:
                kept = out[0]
                for i in range(1, 8):
                    kept = jnp.where(sub == i, out[i], kept)
            else:
                kept = jnp.where(here, 0.0, tile)
                kept = kept - (weighted([cols[j][t] for j in range(4)], out[:4]) + weighted([cols[j][t] for j in range(4, 8)], out[4:]))
            new.append(kept)
        tiles = new
    return tiles, log_det


def weighted(a, b):
    return (a[0] * b[0] + a[1] * b[1]) + (a[2] * b[2] + a[3] * b[3])


def small_step(s, d_ref, ld_ref):
    half, offset = s // 2, (s % 2) * SMALL
    mine, others = slice(128 * half, 128 * half + 128), slice(128 * (1 - half), 128 * (1 - half) + 128)
    at = slice(SMALL * s, SMALL * s + SMALL)
    tiles = [d_ref[SMALL * s + 8 * t:SMALL * s + 8 * t + 8, mine] for t in range(SMALL // 8)]
    tiles, ld = eliminate(tiles, ld_ref[...], offset)
    ld_ref[...] = ld
    panel = jnp.concatenate(tiles, 0)
    gap = jnp.zeros((SMALL, 128), jnp.float32)

    def inside(rows):
        lane = lax.broadcasted_iota(jnp.int32, (rows, 128), 1)
        return (lane >= offset) & (lane < offset + SMALL)

    def padded(x):
        return jnp.concatenate([x, gap] if offset == 0 else [gap, x], 0)

    across = dot_nn(jnp.where(inside(SMALL), panel, 0.0), padded(d_ref[at, others]))
    d_ref[at, :] = jnp.concatenate([panel, across] if half == 0 else [across, panel], 1)
    left = {}
    for r in [(s + 1 + i) % 4 for i in range(3)]:
        rows = slice(SMALL * r, SMALL * r + SMALL)
        own = d_ref[rows, mine]
        left[r] = jnp.where(inside(SMALL), own, 0.0)
        if offset:
            d_ref[rows, others] -= dot_nn(left[r], padded(across))
            d_ref[rows, mine] = jnp.where(inside(SMALL), 0.0, own) - dot_nn(left[r], padded(panel))
        else:
            d_ref[rows, mine] = jnp.where(inside(SMALL), 0.0, own) - dot_nn(left[r], padded(panel))
            d_ref[rows, others] -= dot_nn(left[r], padded(across))


def dot_nt(a, b):
    k = a.shape[1] // 2
    left = jnp.concatenate([a, a[:, :k]], 1)
    right = jnp.concatenate([b[:, :k], b[:, :k], b[:, k:]], 1)
    return lax.dot_general(left, right, (((1,), (1,)), ((), ())), preferred_element_type=jnp.float32)


def rows_of(i):
    return pl.ds(pl.multiple_of(i * BIG, BIG), BIG)


def split_to(ref, at, x):
    high, low = halves(x)
    ref[at, :BIG] = high
    ref[at, BIG:] = low


def others_of(k, count):
    return [lax.rem(k + 1 + i, count) for i in range(count - 1)]


def gain(i, k, x_ref, c_ref, g_ref, w_ref):
    g = dot_nt(c_ref[rows_of(i), :], w_ref[...])
    split_to(g_ref, rows_of(i), g)
    x_ref[rows_of(i), rows_of(k)] = g


def update(u, v, k, x_ref, c_ref, g_ref):
    low, high = jnp.minimum(u, v), jnp.maximum(u, v)
    r, c = jnp.where(low < k, low, high), jnp.where(low < k, high, low)
    x_ref[rows_of(r), rows_of(c)] -= dot_nt(g_ref[rows_of(r), :], c_ref[rows_of(c), :])


def background(k, count, x_ref, c_ref, g_ref, w_ref):
    others = others_of(k, count)

    def turned(j):
        x_ref[rows_of(k), rows_of(j)] = dot_nt(w_ref[...], c_ref[rows_of(j), :])

    first = [functools.partial(gain, i, k, x_ref, c_ref, g_ref, w_ref) for i in others[1:]]
    first += [functools.partial(turned, j) for j in others]
    pairs = [(a, b) for a in range(count - 1) for b in range(a, count - 1) if b > 0]
    rest = [functools.partial(update, others[a], others[b], k, x_ref, c_ref, g_ref) for a, b in pairs]
    share = -(-len(rest) // 3)
    return [first] + [rest[i * share:(i + 1) * share] for i in range(3)]


def boundary(k, x_ref, d_ref, c_ref, g_ref, w_ref):
    count = x_ref.shape[0] // BIG
    q = k + 1
    w = d_ref[...]
    split_to(w_ref, slice(None), w)
    x_ref[rows_of(k), rows_of(k)] = -w
    split_to(c_ref, rows_of(q), x_ref[rows_of(q), rows_of(k)])
    for r in range(0, BIG, SMALL):
        rows = pl.ds(pl.multiple_of(q * BIG + r, SMALL), SMALL)
        split_to(g_ref, rows, dot_nt(c_ref[rows, :], w_ref[...]))
        d_ref[r:r + SMALL, :] = x_ref[rows, rows_of(q)] - dot_nt(g_ref[rows, :], c_ref[rows_of(q), :])
    for i in others_of(k, count)[1:]:
        split_to(c_ref, rows_of(i), x_ref[rows_of(i), rows_of(k)])


def eliminate_blocks(start, stop, x_ref, ld_ref, d_ref, c_ref, g_ref, w_ref):
    count = x_ref.shape[0] // BIG

    def body(q, _):
        boundary(q - 1, x_ref, d_ref, c_ref, g_ref, w_ref)
        work = background(q - 1, count, x_ref, c_ref, g_ref, w_ref)
        for s in range(BIG // SMALL):
            small_step(s, d_ref, ld_ref)
            for unit in work[s]:
                unit()
        return 0

    lax.fori_loop(start, stop, body, 0)


def turned_halves(ref, u):
    split_at = u.shape[0]
    high, low = halves(u.T)
    ref[:, :split_at] = high
    ref[:, split_at:] = low


def blocks_of(size):
    return [slice(i, i + BIG) for i in range(0, size, BIG)]


def stacked(ref, part):
    depth = ref.shape[1] // 2 if part is not None else ref.shape[1]
    at = slice((part or 0) * depth, (part or 0) * depth + depth)
    return jnp.concatenate([ref[m, at, :] for m in range(ref.shape[0])], 0)


def own_columns(size, tile):
    return pl.ds(pl.multiple_of(tile * size, 128), size)


def first_kernel(numbers_ref, prior_ref, other_ref, rows_ref,
                 x_ref, d_ref, ld_ref, row_ref, col_ref, c_ref, g_ref, w_ref, u_ref):
    size = other_ref.shape[0]
    tile = lax.axis_index("tile")
    own_at, other_at = tile * size, (1 - tile) * size
    weight_row, weight = numbers_ref[0:1, :], numbers_ref[0:1, 0:1]
    here = lax.broadcasted_iota(jnp.int32, (128, 128), 0) == lax.broadcasted_iota(jnp.int32, (128, 128), 1)
    for i in range(0, 2 * size, 128):
        at = slice(i % size, i % size + 128)
        square = other_ref[at, at] if i < size else prior_ref[at, pl.ds(pl.multiple_of(own_at + at.start, 128), 128)]
        square = jnp.where(here, square, 0.0)
        row_ref[:, i:i + 128] = lax.rsqrt(weight_row * jnp.sum(square, 0, keepdims=True))
        col_ref[i:i + 128, :] = lax.rsqrt(weight * jnp.sum(square, 1, keepdims=True))
    turned_halves(u_ref, stacked(rows_ref, None) * row_ref[:, :size])
    for i, at in enumerate(blocks_of(size)):
        down_scale = col_ref[at, :] * weight
        low = slice(size + at.start, size + at.stop)
        low_scale = col_ref[low, :] * weight
        for j, to in enumerate(blocks_of(size)):
            if j <= i:
                x_ref[at, to] = other_ref[at, to] * down_scale * row_ref[:, to] + dot_nt(u_ref[at, :], u_ref[to, :])
                far = slice(size + to.start, size + to.stop)
                x_ref[low, far] = prior_ref[at, pl.ds(pl.multiple_of(own_at + to.start, 128), BIG)] * low_scale * row_ref[:, far]
            x_ref[low, to] = prior_ref[at, pl.ds(pl.multiple_of(other_at + to.start, 128), BIG)] * low_scale * row_ref[:, to]
    ld_ref[...] = jnp.zeros_like(ld_ref)
    d_ref[...] = x_ref[:BIG, :BIG]
    for s in range(BIG // SMALL):
        small_step(s, d_ref, ld_ref)
    eliminate_blocks(1, size // BIG, x_ref, ld_ref, d_ref, c_ref, g_ref, w_ref)


def second_kernel(x_in_ref, d_in_ref, ld_in_ref, rows_ref, row_ref, col_ref, gain_row_ref, gain_col_ref,
                  send_ref, own_ref, ld_ref, x_ref, d_ref, c_ref, g_ref, w_ref, u_ref):
    n = x_ref.shape[0]
    size = own_ref.shape[0]
    count = n // BIG
    half = size // BIG
    x_ref[...] = x_in_ref[...]
    d_ref[...] = d_in_ref[...]
    ld_ref[...] = ld_in_ref[...]
    turned_halves(u_ref, stacked(rows_ref, 0) * row_ref[:, size:])
    for i, at in enumerate(blocks_of(size)):
        for j, to in enumerate(blocks_of(size)):
            if j <= i:
                x_ref[size + at.start:size + at.stop, size + to.start:size + to.stop] += dot_nt(u_ref[at, :], u_ref[to, :])
    eliminate_blocks(half, count, x_ref, ld_ref, d_ref, c_ref, g_ref, w_ref)
    k = count - 1
    w = d_ref[...]
    split_to(w_ref, slice(None), w)
    x_ref[k * BIG:n, k * BIG:n] = -w

    tile = lax.axis_index("tile")

    def gains_of(block):
        start = (1 - tile) * size + block * BIG if block < half else tile * size + (block - half) * BIG
        return pl.ds(pl.multiple_of(start, 128), BIG)

    def finish(a, b, value):
        rows, cols = slice(a * BIG, a * BIG + BIG), slice(b * BIG, b * BIG + BIG)
        left = col_ref[rows, :] * gain_col_ref[gains_of(a), :]
        value = -value * left * (row_ref[:, cols] * gain_row_ref[:, gains_of(b)])
        if a < half:
            send_ref[rows, cols] = value
        else:
            own_ref[(a - half) * BIG:(a - half) * BIG + BIG, (b - half) * BIG:(b - half) * BIG + BIG] = value

    total = ld_ref[...] - 2.0 * jnp.sum(jnp.log(row_ref[...]))
    ld_ref[...] = total
    send_ref[size:, :] = jnp.zeros((REG[0], n), jnp.float32)
    send_ref[size:, :REG[1]] = total
    finish(k, k, -w)
    for i in range(k):
        at = slice(i * BIG, i * BIG + BIG)
        c = x_ref[at, k * BIG:n]
        split_to(c_ref, at, c)
        g = dot_nt(c_ref[at, :], w_ref[...])
        split_to(g_ref, at, g)
        finish(i, k, g)
    for a in range(k):
        at = slice(a * BIG, a * BIG + BIG)
        for b in range(a, k):
            to = slice(b * BIG, b * BIG + BIG)
            finish(a, b, x_ref[at, to] - dot_nt(g_ref[at, :], c_ref[to, :]))


def states(n, rows):
    return [
        pltpu.VMEM((n, 2 * BIG), jnp.bfloat16),
        pltpu.VMEM((n, 2 * BIG), jnp.bfloat16),
        pltpu.VMEM((BIG, 2 * BIG), jnp.bfloat16),
        pltpu.VMEM((n // 2, 2 * rows), jnp.bfloat16),
    ]


def in_vmem(count):
    return [pl.BlockSpec(memory_space=pltpu.VMEM)] * count


def first_half(numbers, prior, other, rows):
    size, n = prior.shape
    f32 = jnp.float32
    return pl.pallas_call(
        first_kernel,
        out_shape=(jax.ShapeDtypeStruct((n, n), f32), jax.ShapeDtypeStruct((BIG, BIG), f32), jax.ShapeDtypeStruct(REG, f32),
                   jax.ShapeDtypeStruct((1, n), f32), jax.ShapeDtypeStruct((n, 1), f32)),
        in_specs=in_vmem(4),
        out_specs=tuple(in_vmem(5)),
        scratch_shapes=states(n, rows.shape[0] * rows.shape[1]),
        compiler_params=pltpu.CompilerParams(vmem_limit_bytes=48 << 20),
        cost_estimate=pl.CostEstimate(flops=12 * n**3, bytes_accessed=8 * n * n, transcendentals=0),
    )(numbers, prior, other, rows)


def second_half(x, d, log_det, rows, row, col, gain):
    n = x.shape[0]
    size = n // 2
    f32 = jnp.float32
    return pl.pallas_call(
        second_kernel,
        out_shape=(jax.ShapeDtypeStruct((size + REG[0], n), f32), jax.ShapeDtypeStruct((size, size), f32), jax.ShapeDtypeStruct(REG, f32)),
        in_specs=in_vmem(8),
        out_specs=tuple(in_vmem(3)),
        scratch_shapes=[pltpu.VMEM((n, n), f32), pltpu.VMEM((BIG, BIG), f32)] + states(n, rows.shape[0] * rows.shape[1] // 2),
        compiler_params=pltpu.CompilerParams(vmem_limit_bytes=48 << 20),
        cost_estimate=pl.CostEstimate(flops=12 * n**3, bytes_accessed=8 * n * n, transcendentals=0),
    )(x, d, log_det, rows, row, col, gain[None, :], gain[:, None])


def last_kernel(numbers_ref, first_ref, prior_ref, rows_ref, own_ref, sent_ref, got_ref,
                block_ref, coupling_ref, block_buf, coupling_buf, u_ref, sems):
    size, n = prior_ref.shape
    weight, have_block, got_block, have_coupling, got_coupling = [numbers_ref[i] for i in range(5)]
    own_at = first_ref[0] * size
    cross_at = size - own_at
    turned_halves(u_ref, stacked(rows_ref, 1))
    copies = []
    for i, at in enumerate(blocks_of(size)):
        for j, to in enumerate(blocks_of(size)):
            for which in range(2):
                if which == 0:
                    have = own_ref[at, to] if i <= j else own_ref[to, at].T
                    got = got_ref[at, to] if i <= j else got_ref[to, at].T
                    cols = pl.ds(pl.multiple_of(own_at + j * BIG, BIG), BIG)
                else:
                    have = sent_ref[to, size + at.start:size + at.stop].T
                    got = got_ref[at, size + to.start:size + to.stop]
                    cols = pl.ds(pl.multiple_of(cross_at + j * BIG, BIG), BIG)
                base = weight * prior_ref[at, cols]
                if which == 0:
                    base = base + dot_nt(u_ref[at, :], u_ref[to, :])
                block_buf[at, cols] = base - (have_block * have + got_block * got)
                coupling_buf[at, cols] = have_coupling * have + got_coupling * got
        for o, (buf, ref) in enumerate([(block_buf, block_ref), (coupling_buf, coupling_ref)]):
            copy = pltpu.make_async_copy(buf.at[at], ref.at[at], sems.at[2 * i + o])
            copy.start()
            copies.append(copy)
    for copy in copies:
        copy.wait()


def outputs(numbers, tile, prior, rows, own, sent, got):
    size, n = prior.shape
    f32 = jnp.float32
    return pl.pallas_call(
        last_kernel,
        out_shape=(jax.ShapeDtypeStruct((size, n), f32),) * 2,
        in_specs=[pl.BlockSpec(memory_space=pltpu.SMEM)] * 2 + in_vmem(5),
        out_specs=(pl.BlockSpec(memory_space=pl.ANY),) * 2,
        scratch_shapes=[pltpu.VMEM((size, n), f32)] * 2
        + [pltpu.VMEM((size, rows.shape[0] * rows.shape[1]), jnp.bfloat16), pltpu.SemaphoreType.DMA((2 * size // BIG,))],
        compiler_params=pltpu.CompilerParams(vmem_limit_bytes=48 << 20),
        cost_estimate=pl.CostEstimate(flops=6 * size * size * n, bytes_accessed=20 * size * n, transcendentals=0),
    )(numbers, tile, prior, rows, own, sent, got)


def order_kernel(step_ref, value_ref, weight_ref, first_ref, rest_ref):
    parts = first_ref.shape[0] - 1
    tile = lax.axis_index("tile")
    for k in range(value_ref.shape[0]):
        step = step_ref[k]
        part, odd = lax.shift_right_logical(step, 1), (step & 1) == 1
        rows = value_ref[k] * jnp.sqrt(weight_ref[k])
        before = jnp.where(part == 0, parts - 1, part - 1)
        at_zero, at_one = part, before
        first_ref[jnp.where(odd, parts, jnp.where(tile == 0, at_one, at_zero))] = rows
        rest_ref[2 * jnp.where(odd | (tile == 0), at_zero, at_one) + (step & 1)] = rows


def by_step(values, weights, steps, parts):
    depth, size = values.shape[1:]
    return pl.pallas_call(
        order_kernel,
        out_shape=(jax.ShapeDtypeStruct((parts + 1, depth, size), jnp.float32), jax.ShapeDtypeStruct((2 * parts, depth, size), jnp.float32)),
        in_specs=[
            pl.BlockSpec(memory_space=pltpu.SMEM),
            pl.BlockSpec(memory_space=pltpu.VMEM),
            pl.BlockSpec(memory_space=pltpu.VMEM),
        ],
        out_specs=tuple(in_vmem(2)),
        compiler_params=pltpu.CompilerParams(vmem_limit_bytes=40 << 20),
    )(steps, values, weights[..., None])


def exchange_kernel(time_ref, rho_ref, first_ref, prior_ref, rows_ref, other_ref, numbers_ref, mine_ref, next_ref, send_sems, recv_sems):
    parts = rows_ref.shape[0]
    size = other_ref.shape[0]
    me, tile = lax.axis_index("tm"), lax.axis_index("tile")
    there = 1 - tile
    after, before = lax.rem(me + 1, parts), lax.rem(me + parts - 1, parts)
    mesh = pl.DeviceIdType.MESH
    barrier = pltpu.get_barrier_semaphore()
    for i in range(parts):
        pl.semaphore_signal(barrier, inc=1, device_id=(lax.rem(me + i, parts), there), device_id_type=mesh)
    pl.semaphore_signal(barrier, inc=1, device_id=(after, tile), device_id_type=mesh)
    mine_ref[0:1, :] = jnp.full((1, REG[1]), time_ref[0], jnp.float32)
    mine_ref[1:2, :] = jnp.full((1, REG[1]), rho_ref[0], jnp.float32)
    mine_ref[2:, :] = jnp.zeros((REG[0] - 2, REG[1]), jnp.float32)
    pl.semaphore_wait(barrier, parts + 1)

    def rows_copy(i, slot):
        to = lax.rem(me + i, parts)
        return pltpu.make_async_remote_copy(
            src_ref=first_ref.at[to], dst_ref=rows_ref.at[slot], send_sem=send_sems.at[i],
            recv_sem=recv_sems.at[slot], device_id=(to, there), device_id_type=mesh)

    scalars = pltpu.make_async_remote_copy(
        src_ref=mine_ref, dst_ref=next_ref, send_sem=send_sems.at[parts], recv_sem=recv_sems.at[parts],
        device_id=(before, tile), device_id_type=mesh)
    prior = pltpu.make_async_remote_copy(
        src_ref=prior_ref.at[:, own_columns(size, tile)], dst_ref=other_ref, send_sem=send_sems.at[parts + 1],
        recv_sem=recv_sems.at[parts + 1], device_id=(me, there), device_id_type=mesh)
    scalars.start()
    for i in range(parts - 1, -1, -1):
        rows_copy(i, me).start()
    prior.start()
    scalars.wait()
    last = me == parts - 1
    own, following = mine_ref[...], next_ref[...]
    row = lax.broadcasted_iota(jnp.int32, REG, 0)
    chosen = jnp.where(tile == 0, own, jnp.where(last, 1.0, following))
    numbers_ref[...] = jnp.where(row == 0, chosen, jnp.where(last, 0.0, following))
    for i in range(parts):
        rows_copy(i, me).wait_send()
    for i in range(parts):
        rows_copy(i, lax.rem(me + i, parts)).wait_recv()
    prior.wait()


def exchange(time_diag, rho, first, prior):
    parts = first.shape[0] - 1
    size = prior.shape[0]
    f32 = jnp.float32
    return pl.pallas_call(
        exchange_kernel,
        out_shape=(jax.ShapeDtypeStruct((parts,) + first.shape[1:], f32), jax.ShapeDtypeStruct((size, size), f32), jax.ShapeDtypeStruct(REG, f32)),
        in_specs=[pl.BlockSpec(memory_space=pltpu.SMEM)] * 2 + in_vmem(1) + [pl.BlockSpec(memory_space=pl.ANY)],
        out_specs=tuple(in_vmem(3)),
        scratch_shapes=[pltpu.VMEM(REG, f32)] * 2 + [pltpu.SemaphoreType.DMA((parts + 2,))] * 2,
        compiler_params=pltpu.CompilerParams(collective_id=0, has_side_effects=True, vmem_limit_bytes=16 << 20),
        cost_estimate=pl.CostEstimate(flops=0, bytes_accessed=4 * size * size, transcendentals=0),
    )(time_diag, rho, first, prior)


def on_device(prior_space, node_gain, time_diag, rho, obs_values, obs_weight, obs_step):
    size, node_count = prior_space.shape
    parts = lax.axis_size("tm")
    tile = lax.axis_index("tile")
    first = tile == 0

    def chosen(a, b):
        return jnp.where(first, a, b)

    sent, rest = by_step(obs_values[0], obs_weight[0], obs_step[0, 0], parts)
    rows_other, prior_other, numbers = exchange(time_diag, rho, sent, prior_space)
    rest, rows_other = lax.optimization_barrier((rest, rows_other))
    rest = lax.all_to_all(rest.reshape(parts, -1, size), "tm", split_axis=0, concat_axis=0, tiled=True)

    x, d, log_det, row, col = first_half(numbers, prior_space, prior_other, rows_other)
    send, own, log_det = second_half(x, d, log_det, rest, row, col, node_gain)
    got = lax.ppermute(send, "tile", [(0, 1), (1, 0)])
    interior_logdet = chosen(log_det[0, 0], got[size, 0]).reshape(1) / node_count

    now, following, across = rho[1] * rho[1], numbers[1, 0] * numbers[1, 0], -(rho[0] * rho[1])
    factors = jnp.stack([time_diag[1], chosen(now, following), chosen(following, now), chosen(across, 0.0), chosen(0.0, across)])
    block, coupling = outputs(factors, tile.reshape(1).astype(jnp.int32), prior_space, rest, own, send, got)
    return block[None], coupling[None], interior_logdet


def solution(mesh):
    in_specs = (
        P("tile", None),
        P(),
        P("tm"),
        P("tm"),
        P("tile", "tm", None, None),
        P("tile", "tm", None),
        P("tile", "tm", None),
    )
    out_specs = (P("tm", "tile", None), P("tm", "tile", None), P("tm"))
    return jax.shard_map(
        on_device, mesh=mesh, in_specs=in_specs, out_specs=out_specs, check_vma=False
    )
```

```python
import functools
import jax, jax.numpy as jnp
from jax import lax
from jax.experimental import pallas as pl
from jax.experimental.pallas import tpu as pltpu
from jax.sharding import PartitionSpec as P

REG = (8, 128)
BIG, SMALL = 256, 64


def along(x, j):
    return jnp.broadcast_to(x[:, j:j + 1], REG)


def down(x, i):
    return jnp.take_along_axis(x, jnp.full(REG, i, jnp.int32), axis=0)


def halves(x):
    high = x.astype(jnp.bfloat16)
    return high, (x - high.astype(jnp.float32)).astype(jnp.bfloat16)


def dot_nn(a, b):
    ah, al = halves(a)
    bh, bl = halves(b)
    return jnp.dot(jnp.concatenate([ah, al, ah], 1), jnp.concatenate([bh, bh, bl], 0), preferred_element_type=jnp.float32)


def pair_inverse(a, b, d):
    det = a * d - b * b
    r = 1.0 / det
    return d * r, -(b * r), a * r, det


def inverse_of_four(s):
    a, b, d, det1 = pair_inverse(s[0, 0], s[1, 0], s[1, 1])
    q = [[s[2, 0], s[2, 1]], [s[3, 0], s[3, 1]]]
    m = [[q[i][0] * a + q[i][1] * b, q[i][0] * b + q[i][1] * d] for i in range(2)]
    u = s[2, 2] - (m[0][0] * q[0][0] + m[0][1] * q[0][1])
    v = s[3, 2] - (m[1][0] * q[0][0] + m[1][1] * q[0][1])
    w = s[3, 3] - (m[1][0] * q[1][0] + m[1][1] * q[1][1])
    u, v, w, det2 = pair_inverse(u, v, w)
    low = [[u * m[0][j] + v * m[1][j] for j in range(2)], [v * m[0][j] + w * m[1][j] for j in range(2)]]
    w00 = a + (m[0][0] * low[0][0] + m[1][0] * low[1][0])
    w01 = b + (m[0][0] * low[0][1] + m[1][0] * low[1][1])
    w11 = d + (m[0][1] * low[0][1] + m[1][1] * low[1][1])
    inverse = [[w00, w01, -low[0][0], -low[1][0]],
               [w01, w11, -low[0][1], -low[1][1]],
               [-low[0][0], -low[0][1], u, v],
               [-low[1][0], -low[1][1], v, w]]
    return inverse, det1, det2


def eliminate(tiles, log_det, offset):
    lane = lax.broadcasted_iota(jnp.int32, REG, 1) - offset
    sub = lax.broadcasted_iota(jnp.int32, REG, 0)
    for home in range(len(tiles)):
        p = 8 * home
        cols = [[along(t, offset + p + j) for t in tiles] for j in range(8)]
        c = [cols[j][home] for j in range(8)]
        head, det1, det2 = inverse_of_four({(i, j): down(c[j], i) for j in range(4) for i in range(j, 4)})
        slope = [weighted([head[i][j] for i in range(4)], c[:4]) for j in range(4)]
        rest = [c[j] - weighted([down(c[j], i) for i in range(4)], slope) for j in range(4, 8)]
        foot, det3, det4 = inverse_of_four({(i, j): down(rest[j], i + 4) for j in range(4) for i in range(j, 4)})
        log_det = log_det + ((jnp.log(det1) + jnp.log(det2)) + (jnp.log(det3) + jnp.log(det4)))
        here = (lane >= p) & (lane < p + 8)
        rows = jnp.where(here, jnp.where(lane == p + sub, 1.0, 0.0), tiles[home])
        top = [down(rows, i) for i in range(4)]
        upper = [weighted(head[i], top) for i in range(4)]
        rows = rows - weighted(c[:4], upper)
        low = [down(rows, i) for i in range(4, 8)]
        lower = [weighted(foot[i], low) for i in range(4)]
        upper = [upper[i] - weighted([down(slope[i], j) for j in range(4, 8)], lower) for i in range(4)]
        out = upper + lower
        new = []
        for t, tile in enumerate(tiles):
            if t == home:
                kept = out[0]
                for i in range(1, 8):
                    kept = jnp.where(sub == i, out[i], kept)
            else:
                kept = jnp.where(here, 0.0, tile)
                kept = kept - (weighted([cols[j][t] for j in range(4)], out[:4]) + weighted([cols[j][t] for j in range(4, 8)], out[4:]))
            new.append(kept)
        tiles = new
    return tiles, log_det


def weighted(a, b):
    return (a[0] * b[0] + a[1] * b[1]) + (a[2] * b[2] + a[3] * b[3])


def small_step(s, d_ref, ld_ref):
    half, offset = s // 2, (s % 2) * SMALL
    mine, others = slice(128 * half, 128 * half + 128), slice(128 * (1 - half), 128 * (1 - half) + 128)
    at = slice(SMALL * s, SMALL * s + SMALL)
    tiles = [d_ref[SMALL * s + 8 * t:SMALL * s + 8 * t + 8, mine] for t in range(SMALL // 8)]
    tiles, ld = eliminate(tiles, ld_ref[...], offset)
    ld_ref[...] = ld
    panel = jnp.concatenate(tiles, 0)
    gap = jnp.zeros((SMALL, 128), jnp.float32)

    def inside(rows):
        lane = lax.broadcasted_iota(jnp.int32, (rows, 128), 1)
        return (lane >= offset) & (lane < offset + SMALL)

    def padded(x):
        return jnp.concatenate([x, gap] if offset == 0 else [gap, x], 0)

    across = dot_nn(jnp.where(inside(SMALL), panel, 0.0), padded(d_ref[at, others]))
    d_ref[at, :] = jnp.concatenate([panel, across] if half == 0 else [across, panel], 1)
    left = {}
    for r in [(s + 1 + i) % 4 for i in range(3)]:
        rows = slice(SMALL * r, SMALL * r + SMALL)
        own = d_ref[rows, mine]
        left[r] = jnp.where(inside(SMALL), own, 0.0)
        if offset:
            d_ref[rows, others] -= dot_nn(left[r], padded(across))
            d_ref[rows, mine] = jnp.where(inside(SMALL), 0.0, own) - dot_nn(left[r], padded(panel))
        else:
            d_ref[rows, mine] = jnp.where(inside(SMALL), 0.0, own) - dot_nn(left[r], padded(panel))
            d_ref[rows, others] -= dot_nn(left[r], padded(across))


def dot_nt(a, b):
    k = a.shape[1] // 2
    left = jnp.concatenate([a, a[:, :k]], 1)
    right = jnp.concatenate([b[:, :k], b[:, :k], b[:, k:]], 1)
    return lax.dot_general(left, right, (((1,), (1,)), ((), ())), preferred_element_type=jnp.float32)


def rows_of(i):
    return pl.ds(pl.multiple_of(i * BIG, BIG), BIG)


def split_to(ref, at, x):
    high, low = halves(x)
    ref[at, :BIG] = high
    ref[at, BIG:] = low


def others_of(k, count):
    return [lax.rem(k + 1 + i, count) for i in range(count - 1)]


def gain(i, k, x_ref, c_ref, g_ref, w_ref):
    g = dot_nt(c_ref[rows_of(i), :], w_ref[...])
    split_to(g_ref, rows_of(i), g)
    x_ref[rows_of(i), rows_of(k)] = g


def update(u, v, k, x_ref, c_ref, g_ref):
    low, high = jnp.minimum(u, v), jnp.maximum(u, v)
    r, c = jnp.where(low < k, low, high), jnp.where(low < k, high, low)
    x_ref[rows_of(r), rows_of(c)] -= dot_nt(g_ref[rows_of(r), :], c_ref[rows_of(c), :])


def background(k, count, x_ref, c_ref, g_ref, w_ref):
    others = others_of(k, count)

    def turned(j):
        x_ref[rows_of(k), rows_of(j)] = dot_nt(w_ref[...], c_ref[rows_of(j), :])

    first = [functools.partial(gain, i, k, x_ref, c_ref, g_ref, w_ref) for i in others[1:]]
    first += [functools.partial(turned, j) for j in others]
    pairs = [(a, b) for a in range(count - 1) for b in range(a, count - 1) if b > 0]
    rest = [functools.partial(update, others[a], others[b], k, x_ref, c_ref, g_ref) for a, b in pairs]
    share = -(-len(rest) // 3)
    return [first] + [rest[i * share:(i + 1) * share] for i in range(3)]


def boundary(k, x_ref, d_ref, c_ref, g_ref, w_ref):
    count = x_ref.shape[0] // BIG
    q = k + 1
    w = d_ref[...]
    split_to(w_ref, slice(None), w)
    x_ref[rows_of(k), rows_of(k)] = -w
    split_to(c_ref, rows_of(q), x_ref[rows_of(q), rows_of(k)])
    for r in range(0, BIG, SMALL):
        rows = pl.ds(pl.multiple_of(q * BIG + r, SMALL), SMALL)
        split_to(g_ref, rows, dot_nt(c_ref[rows, :], w_ref[...]))
        d_ref[r:r + SMALL, :] = x_ref[rows, rows_of(q)] - dot_nt(g_ref[rows, :], c_ref[rows_of(q), :])
    for i in others_of(k, count)[1:]:
        split_to(c_ref, rows_of(i), x_ref[rows_of(i), rows_of(k)])


def eliminate_blocks(start, stop, x_ref, ld_ref, d_ref, c_ref, g_ref, w_ref):
    count = x_ref.shape[0] // BIG

    def body(q, _):
        boundary(q - 1, x_ref, d_ref, c_ref, g_ref, w_ref)
        work = background(q - 1, count, x_ref, c_ref, g_ref, w_ref)
        for s in range(BIG // SMALL):
            small_step(s, d_ref, ld_ref)
            for unit in work[s]:
                unit()
        return 0

    lax.fori_loop(start, stop, body, 0)


def turned_halves(ref, u):
    split_at = u.shape[0]
    high, low = halves(u.T)
    ref[:, :split_at] = high
    ref[:, split_at:] = low


def blocks_of(size):
    return [slice(i, i + BIG) for i in range(0, size, BIG)]


def stacked(ref, part):
    depth = ref.shape[1] // 2 if part is not None else ref.shape[1]
    at = slice((part or 0) * depth, (part or 0) * depth + depth)
    return jnp.concatenate([ref[m, at, :] for m in range(ref.shape[0])], 0)


def own_columns(size, tile):
    return pl.ds(pl.multiple_of(tile * size, 128), size)


def column_of(row):
    here = lax.broadcasted_iota(jnp.int32, (128, 128), 0) == lax.broadcasted_iota(jnp.int32, (128, 128), 1)
    parts = [jnp.sum(jnp.where(here, row[:, i:i + 128], 0.0), 1, keepdims=True) for i in range(0, row.shape[1], 128)]
    return jnp.concatenate(parts, 0)


def first_kernel(numbers_ref, prior_ref, other_in_ref, rows_ref,
                 x_ref, d_ref, ld_ref, row_ref, c_ref, g_ref, w_ref, u_ref, col_ref, other_ref, in_sem):
    size = other_ref.shape[0]
    fetch = pltpu.make_async_copy(other_in_ref.at[:, :size], other_ref, in_sem)
    fetch.start()
    fetch.wait()
    tile = lax.axis_index("tile")
    own_at, other_at = tile * size, (1 - tile) * size
    weight_row, weight = numbers_ref[0:1, :], numbers_ref[0:1, 0:1]
    here = lax.broadcasted_iota(jnp.int32, (128, 128), 0) == lax.broadcasted_iota(jnp.int32, (128, 128), 1)
    for i in range(0, 2 * size, 128):
        at = slice(i % size, i % size + 128)
        square = other_ref[at, at] if i < size else prior_ref[at, pl.ds(pl.multiple_of(own_at + at.start, 128), 128)]
        square = jnp.where(here, square, 0.0)
        row_ref[:, i:i + 128] = lax.rsqrt(weight_row * jnp.sum(square, 0, keepdims=True))
    col_ref[...] = column_of(row_ref[...])
    turned_halves(u_ref, stacked(rows_ref, None) * row_ref[:, :size])
    for i, at in enumerate(blocks_of(size)):
        down_scale = col_ref[at, :] * weight
        low = slice(size + at.start, size + at.stop)
        low_scale = col_ref[low, :] * weight
        for j, to in enumerate(blocks_of(size)):
            if j <= i:
                x_ref[at, to] = other_ref[at, to] * down_scale * row_ref[:, to] + dot_nt(u_ref[at, :], u_ref[to, :])
                far = slice(size + to.start, size + to.stop)
                x_ref[low, far] = prior_ref[at, pl.ds(pl.multiple_of(own_at + to.start, 128), BIG)] * low_scale * row_ref[:, far]
            x_ref[low, to] = prior_ref[at, pl.ds(pl.multiple_of(other_at + to.start, 128), BIG)] * low_scale * row_ref[:, to]
    ld_ref[...] = jnp.zeros_like(ld_ref)
    d_ref[...] = x_ref[:BIG, :BIG]
    for s in range(BIG // SMALL):
        small_step(s, d_ref, ld_ref)
    eliminate_blocks(1, size // BIG, x_ref, ld_ref, d_ref, c_ref, g_ref, w_ref)


def second_kernel(x_in_ref, d_in_ref, ld_in_ref, rows_ref, row_ref, gain_ref,
                  send_out_ref, own_out_ref, x_ref, d_ref, c_ref, g_ref, w_ref, u_ref, left_ref, left_col_ref, ld_ref,
                  send_ref, own_ref, in_sem, out_sems):
    n = x_ref.shape[0]
    size = own_ref.shape[0]
    count = n // BIG
    half = size // BIG
    fetch = pltpu.make_async_copy(x_in_ref, x_ref, in_sem)
    fetch.start()
    d_ref[...] = d_in_ref[...]
    ld_ref[...] = ld_in_ref[...]
    turned_halves(u_ref, stacked(rows_ref, 0) * row_ref[:, size:])
    tile = lax.axis_index("tile")
    left_ref[:, :size] = row_ref[:, :size] * gain_ref[:, own_columns(size, 1 - tile)]
    left_ref[:, size:] = row_ref[:, size:] * gain_ref[:, own_columns(size, tile)]
    left_col_ref[...] = column_of(left_ref[...])
    fetch.wait()
    for i, at in enumerate(blocks_of(size)):
        for j, to in enumerate(blocks_of(size)):
            if j <= i:
                x_ref[size + at.start:size + at.stop, size + to.start:size + to.stop] += dot_nt(u_ref[at, :], u_ref[to, :])
    eliminate_blocks(half, count, x_ref, ld_ref, d_ref, c_ref, g_ref, w_ref)
    k = count - 1
    w = d_ref[...]
    split_to(w_ref, slice(None), w)

    def finish(a, b, value):
        rows, cols = slice(a * BIG, a * BIG + BIG), slice(b * BIG, b * BIG + BIG)
        value = -value * left_col_ref[rows, :] * left_ref[:, cols]
        if a < half:
            send_ref[rows, cols] = value
        else:
            own_ref[(a - half) * BIG:(a - half) * BIG + BIG, (b - half) * BIG:(b - half) * BIG + BIG] = value

    send_ref[size:, :] = jnp.zeros((REG[0], n), jnp.float32)
    total = ld_ref[...] - 2.0 * jnp.sum(jnp.log(row_ref[...]))
    send_ref[size:, :REG[1]] = total
    send_ref[size:, size:size + REG[1]] = total
    finish(k, k, -w)
    for i in range(k):
        at = slice(i * BIG, i * BIG + BIG)
        c = x_ref[at, k * BIG:n]
        split_to(c_ref, at, c)
        g = dot_nt(c_ref[at, :], w_ref[...])
        split_to(g_ref, at, g)
        finish(i, k, g)
    copies = []
    for a in range(k + 1):
        at = slice(a * BIG, a * BIG + BIG)
        for b in range(a, k):
            to = slice(b * BIG, b * BIG + BIG)
            finish(a, b, x_ref[at, to] - dot_nt(g_ref[at, :], c_ref[to, :]))
        if a < half:
            rows = slice(a * BIG, a * BIG + BIG if a < half - 1 else size + REG[0])
            copies.append(pltpu.make_async_copy(send_ref.at[rows], send_out_ref.at[rows], out_sems.at[a]))
        else:
            rows = slice((a - half) * BIG, (a - half) * BIG + BIG)
            copies.append(pltpu.make_async_copy(own_ref.at[rows], own_out_ref.at[rows, :size], out_sems.at[a]))
        copies[-1].start()
    for copy in copies:
        copy.wait()


def states(n, rows):
    return [
        pltpu.VMEM((n, 2 * BIG), jnp.bfloat16),
        pltpu.VMEM((n, 2 * BIG), jnp.bfloat16),
        pltpu.VMEM((BIG, 2 * BIG), jnp.bfloat16),
        pltpu.VMEM((n // 2, 2 * rows), jnp.bfloat16),
    ]


def in_vmem(count):
    return [pl.BlockSpec(memory_space=pltpu.VMEM)] * count


def in_hbm(count):
    return [pl.BlockSpec(memory_space=pltpu.HBM)] * count


def first_half(numbers, prior, other, rows):
    size, n = prior.shape
    f32 = jnp.float32
    return pl.pallas_call(
        first_kernel,
        out_shape=(jax.ShapeDtypeStruct((n, n), f32), jax.ShapeDtypeStruct((BIG, BIG), f32), jax.ShapeDtypeStruct(REG, f32),
                   jax.ShapeDtypeStruct((1, n), f32)),
        in_specs=in_vmem(2) + in_hbm(1) + in_vmem(1),
        out_specs=tuple(in_vmem(4)),
        scratch_shapes=states(n, rows.shape[0] * rows.shape[1]) + [pltpu.VMEM((n, 1), f32), pltpu.VMEM((size, size), f32), pltpu.SemaphoreType.DMA],
        compiler_params=pltpu.CompilerParams(vmem_limit_bytes=44 << 20),
        cost_estimate=pl.CostEstimate(flops=12 * n**3, bytes_accessed=8 * n * n, transcendentals=0),
    )(numbers, prior, other, rows)


def second_half(x, d, log_det, rows, row, gain):
    n = x.shape[0]
    size = n // 2
    f32 = jnp.float32
    return pl.pallas_call(
        second_kernel,
        out_shape=(jax.ShapeDtypeStruct((size + REG[0], n), f32), jax.ShapeDtypeStruct((size, n), f32)),
        in_specs=in_hbm(1) + in_vmem(5),
        out_specs=tuple(in_hbm(2)),
        scratch_shapes=[pltpu.VMEM((n, n), f32), pltpu.VMEM((BIG, BIG), f32)] + states(n, rows.shape[0] * rows.shape[1] // 2)
        + [pltpu.VMEM((1, n), f32), pltpu.VMEM((n, 1), f32), pltpu.VMEM(REG, f32), pltpu.VMEM((size + REG[0], n), f32),
           pltpu.VMEM((size, size), f32), pltpu.SemaphoreType.DMA, pltpu.SemaphoreType.DMA((n // BIG,))],
        compiler_params=pltpu.CompilerParams(vmem_limit_bytes=48 << 20),
        cost_estimate=pl.CostEstimate(flops=12 * n**3, bytes_accessed=8 * n * n, transcendentals=0),
    )(x, d, log_det, rows, row, gain[None, :])


def last_kernel(numbers_ref, prior_in_ref, rows_ref, own_in_ref, sent_in_ref, got_in_ref,
                block_ref, coupling_ref, log_ref, prior_ref, own_ref, sent_ref, got_ref, block_buf, coupling_buf, u_ref, in_sems, sems):
    size, n = prior_ref.shape
    tile = lax.axis_index("tile")
    own_at = tile * size
    cross_at = size - own_at
    blocks = blocks_of(size)
    tail = slice(size, size + REG[0])
    fetches = [pltpu.make_async_copy(own_in_ref.at[:, :size], own_ref, in_sems.at[0]),
               pltpu.make_async_copy(sent_in_ref.at[:, size:], sent_ref, in_sems.at[1])]
    for i, at in enumerate(blocks):
        fetches.append(pltpu.make_async_copy(got_in_ref.at[at], got_ref.at[at], in_sems.at[2 + 2 * i]))
        fetches.append(pltpu.make_async_copy(prior_in_ref.at[at], prior_ref.at[at], in_sems.at[3 + 2 * i]))
    fetches.append(pltpu.make_async_copy(got_in_ref.at[tail], got_ref.at[tail], in_sems.at[2 + 2 * len(blocks)]))
    for fetch in fetches:
        fetch.start()
    weight, have_block, got_block, have_coupling, got_coupling = [numbers_ref[i] for i in range(5)]
    turned_halves(u_ref, stacked(rows_ref, 1))
    copies = []
    for i, at in enumerate(blocks):
        for fetch in (fetches[:4] if i == 0 else fetches[2 + 2 * i:4 + 2 * i]):
            fetch.wait()
        for j, to in enumerate(blocks):
            for which in range(2):
                if which == 0:
                    have = own_ref[at, to] if i <= j else own_ref[to, at].T
                    got = got_ref[at, to] if i <= j else got_ref[to, at].T
                    cols = pl.ds(pl.multiple_of(own_at + j * BIG, BIG), BIG)
                else:
                    have = sent_ref[to, at].T
                    got = got_ref[at, size + to.start:size + to.stop]
                    cols = pl.ds(pl.multiple_of(cross_at + j * BIG, BIG), BIG)
                base = weight * prior_ref[at, cols]
                if which == 0:
                    base = base + dot_nt(u_ref[at, :], u_ref[to, :])
                block_buf[at, cols] = base - (have_block * have + got_block * got)
                coupling_buf[at, cols] = have_coupling * have + got_coupling * got
        for o, (buf, ref) in enumerate([(block_buf, block_ref), (coupling_buf, coupling_ref)]):
            copy = pltpu.make_async_copy(buf.at[at], ref.at[at], sems.at[2 * i + o])
            copy.start()
            copies.append(copy)
    fetches[-1].wait()
    log_ref[...] = jnp.where(tile == 0, sent_ref[size:, :REG[1]], got_ref[size:, :REG[1]]) / n
    for copy in copies:
        copy.wait()


def outputs(numbers, prior, rows, own, sent, got):
    size, n = prior.shape
    f32 = jnp.float32
    count = size // BIG
    return pl.pallas_call(
        last_kernel,
        out_shape=(jax.ShapeDtypeStruct((size, n), f32),) * 2 + (jax.ShapeDtypeStruct(REG, f32),),
        in_specs=[pl.BlockSpec(memory_space=pltpu.SMEM)] + in_hbm(1) + in_vmem(1) + in_hbm(3),
        out_specs=tuple(in_hbm(2) + in_vmem(1)),
        scratch_shapes=[pltpu.VMEM((size, n), f32), pltpu.VMEM((size, size), f32), pltpu.VMEM((size + REG[0], size), f32),
                        pltpu.VMEM((size + REG[0], n), f32)] + [pltpu.VMEM((size, n), f32)] * 2
        + [pltpu.VMEM((size, rows.shape[0] * rows.shape[1]), jnp.bfloat16), pltpu.SemaphoreType.DMA((2 * count + 3,)),
           pltpu.SemaphoreType.DMA((2 * count,))],
        compiler_params=pltpu.CompilerParams(vmem_limit_bytes=48 << 20),
        cost_estimate=pl.CostEstimate(flops=6 * size * size * n, bytes_accessed=20 * size * n, transcendentals=0),
    )(numbers, prior, rows, own, sent, got)


def order_kernel(step_ref, value_ref, weight_ref, first_ref, rest_ref):
    parts = first_ref.shape[0] - 1
    tile = lax.axis_index("tile")
    root = jnp.sqrt(weight_ref[...]).T
    for k in range(value_ref.shape[0]):
        step = step_ref[k]
        part, odd = lax.shift_right_logical(step, 1), (step & 1) == 1
        rows = value_ref[k] * root[:, k:k + 1]
        before = jnp.where(part == 0, parts - 1, part - 1)
        at_zero, at_one = part, before
        first_ref[jnp.where(odd, parts, jnp.where(tile == 0, at_one, at_zero))] = rows
        rest_ref[2 * jnp.where(odd | (tile == 0), at_zero, at_one) + (step & 1)] = rows


def by_step(values, weights, steps, parts):
    depth, size = values.shape[1:]
    return pl.pallas_call(
        order_kernel,
        out_shape=(jax.ShapeDtypeStruct((parts + 1, depth, size), jnp.float32), jax.ShapeDtypeStruct((2 * parts, depth, size), jnp.float32)),
        in_specs=[
            pl.BlockSpec(memory_space=pltpu.SMEM),
            pl.BlockSpec(memory_space=pltpu.VMEM),
            pl.BlockSpec(memory_space=pltpu.VMEM),
        ],
        out_specs=tuple(in_vmem(2)),
        compiler_params=pltpu.CompilerParams(vmem_limit_bytes=40 << 20),
    )(steps, values, weights)


def exchange_kernel(time_ref, rho_ref, first_ref, prior_ref, rows_ref, other_ref, numbers_ref, mine_ref, next_ref, send_sems, recv_sems):
    parts = rows_ref.shape[0]
    size = prior_ref.shape[0]
    me, tile = lax.axis_index("tm"), lax.axis_index("tile")
    there = 1 - tile
    after, before = lax.rem(me + 1, parts), lax.rem(me + parts - 1, parts)
    mesh = pl.DeviceIdType.MESH
    barrier = pltpu.get_barrier_semaphore()
    for i in range(parts):
        pl.semaphore_signal(barrier, inc=1, device_id=(lax.rem(me + i, parts), there), device_id_type=mesh)
    pl.semaphore_signal(barrier, inc=1, device_id=(after, tile), device_id_type=mesh)
    mine_ref[0:1, :] = jnp.full((1, REG[1]), time_ref[0], jnp.float32)
    mine_ref[1:2, :] = jnp.full((1, REG[1]), rho_ref[0], jnp.float32)
    mine_ref[2:, :] = jnp.zeros((REG[0] - 2, REG[1]), jnp.float32)
    pl.semaphore_wait(barrier, parts + 1)

    def rows_copy(i, slot):
        to = lax.rem(me + i, parts)
        return pltpu.make_async_remote_copy(
            src_ref=first_ref.at[to], dst_ref=rows_ref.at[slot], send_sem=send_sems.at[i],
            recv_sem=recv_sems.at[slot], device_id=(to, there), device_id_type=mesh)

    scalars = pltpu.make_async_remote_copy(
        src_ref=mine_ref, dst_ref=next_ref, send_sem=send_sems.at[parts], recv_sem=recv_sems.at[parts],
        device_id=(before, tile), device_id_type=mesh)
    prior = pltpu.make_async_remote_copy(
        src_ref=prior_ref.at[:, own_columns(size, tile)], dst_ref=other_ref.at[:, :size], send_sem=send_sems.at[parts + 1],
        recv_sem=recv_sems.at[parts + 1], device_id=(me, there), device_id_type=mesh)
    scalars.start()
    for i in range(parts - 1, -1, -1):
        rows_copy(i, me).start()
    prior.start()
    scalars.wait()
    last = me == parts - 1
    own, following = mine_ref[...], next_ref[...]
    row = lax.broadcasted_iota(jnp.int32, REG, 0)
    chosen = jnp.where(tile == 0, own, jnp.where(last, 1.0, following))
    numbers_ref[...] = jnp.where(row == 0, chosen, jnp.where(last, 0.0, following))
    for i in range(parts):
        rows_copy(i, me).wait_send()
    for i in range(parts):
        rows_copy(i, lax.rem(me + i, parts)).wait_recv()
    prior.wait()


def exchange(time_diag, rho, first, prior):
    parts = first.shape[0] - 1
    size = prior.shape[0]
    f32 = jnp.float32
    return pl.pallas_call(
        exchange_kernel,
        out_shape=(jax.ShapeDtypeStruct((parts,) + first.shape[1:], f32), jax.ShapeDtypeStruct(prior.shape, f32), jax.ShapeDtypeStruct(REG, f32)),
        in_specs=[pl.BlockSpec(memory_space=pltpu.SMEM)] * 2 + in_vmem(1) + in_hbm(1),
        out_specs=tuple(in_vmem(1) + in_hbm(1) + in_vmem(1)),
        scratch_shapes=[pltpu.VMEM(REG, f32)] * 2 + [pltpu.SemaphoreType.DMA((parts + 2,))] * 2,
        compiler_params=pltpu.CompilerParams(collective_id=0, has_side_effects=True, vmem_limit_bytes=16 << 20),
        cost_estimate=pl.CostEstimate(flops=0, bytes_accessed=4 * size * size, transcendentals=0),
    )(time_diag, rho, first, prior)


def on_device(prior_space, node_gain, time_diag, rho, obs_values, obs_weight, obs_step):
    size = prior_space.shape[0]
    parts = lax.axis_size("tm")
    tile = lax.axis_index("tile")
    first = tile == 0

    def chosen(a, b):
        return jnp.where(first, a, b)

    sent, rest = by_step(obs_values[0], obs_weight[0], obs_step[0, 0], parts)
    rows_other, prior_other, numbers = exchange(time_diag, rho, sent, prior_space)
    rest, rows_other = lax.optimization_barrier((rest, rows_other))
    rest = lax.all_to_all(rest.reshape(parts, -1, size), "tm", split_axis=0, concat_axis=0, tiled=True)

    x, d, log_det, row = first_half(numbers, prior_space, prior_other, rows_other)
    send, own = second_half(x, d, log_det, rest, row, node_gain)
    got = lax.ppermute(send, "tile", [(0, 1), (1, 0)])

    now, following, across = rho[1] * rho[1], numbers[1, 0] * numbers[1, 0], -(rho[0] * rho[1])
    factors = jnp.stack([time_diag[1], chosen(now, following), chosen(following, now), chosen(across, 0.0), chosen(0.0, across)])
    block, coupling, log_det = outputs(factors, prior_space, rest, own, send, got)
    return block[None], coupling[None], log_det[0, :1]


def solution(mesh):
    in_specs = (
        P("tile", None),
        P(),
        P("tm"),
        P("tm"),
        P("tile", "tm", None, None),
        P("tile", "tm", None),
        P("tile", "tm", None),
    )
    out_specs = (P("tm", "tile", None), P("tm", "tile", None), P("tm"))
    return jax.shard_map(
        on_device, mesh=mesh, in_specs=in_specs, out_specs=out_specs, check_vma=False
    )
```

```python
import functools
import jax, jax.numpy as jnp
from jax import lax
from jax.experimental import pallas as pl
from jax.experimental.pallas import tpu as pltpu
from jax.sharding import PartitionSpec as P

REG = (8, 128)
BIG, SMALL = 256, 64


def along(x, j):
    return jnp.broadcast_to(x[:, j:j + 1], REG)


def down(x, i):
    return jnp.take_along_axis(x, jnp.full(REG, i, jnp.int32), axis=0)


def halves(x):
    high = x.astype(jnp.bfloat16)
    return high, (x - high.astype(jnp.float32)).astype(jnp.bfloat16)


def dot_nn(a, b):
    ah, al = halves(a)
    bh, bl = halves(b)
    return jnp.dot(jnp.concatenate([ah, al, ah], 1), jnp.concatenate([bh, bh, bl], 0), preferred_element_type=jnp.float32)


def pair_inverse(a, b, d):
    det = a * d - b * b
    r = 1.0 / det
    return d * r, -(b * r), a * r, det


def inverse_of_four(s):
    a, b, d, det1 = pair_inverse(s[0, 0], s[1, 0], s[1, 1])
    q = [[s[2, 0], s[2, 1]], [s[3, 0], s[3, 1]]]
    m = [[q[i][0] * a + q[i][1] * b, q[i][0] * b + q[i][1] * d] for i in range(2)]
    u = s[2, 2] - (m[0][0] * q[0][0] + m[0][1] * q[0][1])
    v = s[3, 2] - (m[1][0] * q[0][0] + m[1][1] * q[0][1])
    w = s[3, 3] - (m[1][0] * q[1][0] + m[1][1] * q[1][1])
    u, v, w, det2 = pair_inverse(u, v, w)
    low = [[u * m[0][j] + v * m[1][j] for j in range(2)], [v * m[0][j] + w * m[1][j] for j in range(2)]]
    w00 = a + (m[0][0] * low[0][0] + m[1][0] * low[1][0])
    w01 = b + (m[0][0] * low[0][1] + m[1][0] * low[1][1])
    w11 = d + (m[0][1] * low[0][1] + m[1][1] * low[1][1])
    inverse = [[w00, w01, -low[0][0], -low[1][0]],
               [w01, w11, -low[0][1], -low[1][1]],
               [-low[0][0], -low[0][1], u, v],
               [-low[1][0], -low[1][1], v, w]]
    return inverse, det1, det2


def eliminate(tiles, log_det, offset):
    lane = lax.broadcasted_iota(jnp.int32, REG, 1) - offset
    sub = lax.broadcasted_iota(jnp.int32, REG, 0)
    for home in range(len(tiles)):
        p = 8 * home
        cols = [[along(t, offset + p + j) for t in tiles] for j in range(8)]
        c = [cols[j][home] for j in range(8)]
        head, det1, det2 = inverse_of_four({(i, j): down(c[j], i) for j in range(4) for i in range(j, 4)})
        slope = [weighted([head[i][j] for i in range(4)], c[:4]) for j in range(4)]
        rest = [c[j] - weighted([down(c[j], i) for i in range(4)], slope) for j in range(4, 8)]
        foot, det3, det4 = inverse_of_four({(i, j): down(rest[j], i + 4) for j in range(4) for i in range(j, 4)})
        log_det = log_det + ((jnp.log(det1) + jnp.log(det2)) + (jnp.log(det3) + jnp.log(det4)))
        here = (lane >= p) & (lane < p + 8)
        rows = jnp.where(here, jnp.where(lane == p + sub, 1.0, 0.0), tiles[home])
        top = [down(rows, i) for i in range(4)]
        upper = [weighted(head[i], top) for i in range(4)]
        rows = rows - weighted(c[:4], upper)
        low = [down(rows, i) for i in range(4, 8)]
        lower = [weighted(foot[i], low) for i in range(4)]
        upper = [upper[i] - weighted([down(slope[i], j) for j in range(4, 8)], lower) for i in range(4)]
        out = upper + lower
        new = []
        for t, tile in enumerate(tiles):
            if t == home:
                kept = out[0]
                for i in range(1, 8):
                    kept = jnp.where(sub == i, out[i], kept)
            else:
                kept = jnp.where(here, 0.0, tile)
                kept = kept - (weighted([cols[j][t] for j in range(4)], out[:4]) + weighted([cols[j][t] for j in range(4, 8)], out[4:]))
            new.append(kept)
        tiles = new
    return tiles, log_det


def weighted(a, b):
    return (a[0] * b[0] + a[1] * b[1]) + (a[2] * b[2] + a[3] * b[3])


def small_step(s, d_ref, ld_ref):
    half, offset = s // 2, (s % 2) * SMALL
    mine, others = slice(128 * half, 128 * half + 128), slice(128 * (1 - half), 128 * (1 - half) + 128)
    at = slice(SMALL * s, SMALL * s + SMALL)
    tiles = [d_ref[SMALL * s + 8 * t:SMALL * s + 8 * t + 8, mine] for t in range(SMALL // 8)]
    tiles, ld = eliminate(tiles, ld_ref[...], offset)
    ld_ref[...] = ld
    panel = jnp.concatenate(tiles, 0)
    gap = jnp.zeros((SMALL, 128), jnp.float32)

    def inside(rows):
        lane = lax.broadcasted_iota(jnp.int32, (rows, 128), 1)
        return (lane >= offset) & (lane < offset + SMALL)

    def padded(x):
        return jnp.concatenate([x, gap] if offset == 0 else [gap, x], 0)

    across = dot_nn(jnp.where(inside(SMALL), panel, 0.0), padded(d_ref[at, others]))
    d_ref[at, :] = jnp.concatenate([panel, across] if half == 0 else [across, panel], 1)
    left = {}
    for r in [(s + 1 + i) % 4 for i in range(3)]:
        rows = slice(SMALL * r, SMALL * r + SMALL)
        own = d_ref[rows, mine]
        left[r] = jnp.where(inside(SMALL), own, 0.0)
        if offset:
            d_ref[rows, others] -= dot_nn(left[r], padded(across))
            d_ref[rows, mine] = jnp.where(inside(SMALL), 0.0, own) - dot_nn(left[r], padded(panel))
        else:
            d_ref[rows, mine] = jnp.where(inside(SMALL), 0.0, own) - dot_nn(left[r], padded(panel))
            d_ref[rows, others] -= dot_nn(left[r], padded(across))


def dot_nt(a, b):
    k = a.shape[1] // 2
    left = jnp.concatenate([a, a[:, :k]], 1)
    right = jnp.concatenate([b[:, :k], b[:, :k], b[:, k:]], 1)
    return lax.dot_general(left, right, (((1,), (1,)), ((), ())), preferred_element_type=jnp.float32)


def rows_of(i):
    return pl.ds(pl.multiple_of(i * BIG, BIG), BIG)


def split_to(ref, at, x):
    high, low = halves(x)
    ref[at, :BIG] = high
    ref[at, BIG:] = low


def others_of(k, count):
    return [lax.rem(k + 1 + i, count) for i in range(count - 1)]


def gain(i, k, x_ref, c_ref, g_ref, w_ref):
    g = dot_nt(c_ref[rows_of(i), :], w_ref[...])
    split_to(g_ref, rows_of(i), g)
    x_ref[rows_of(i), rows_of(k)] = g


def update(u, v, k, x_ref, c_ref, g_ref):
    low, high = jnp.minimum(u, v), jnp.maximum(u, v)
    r, c = jnp.where(low < k, low, high), jnp.where(low < k, high, low)
    x_ref[rows_of(r), rows_of(c)] -= dot_nt(g_ref[rows_of(r), :], c_ref[rows_of(c), :])


def background(k, count, x_ref, c_ref, g_ref, w_ref):
    others = others_of(k, count)

    def turned(j):
        x_ref[rows_of(k), rows_of(j)] = dot_nt(w_ref[...], c_ref[rows_of(j), :])

    first = [functools.partial(gain, i, k, x_ref, c_ref, g_ref, w_ref) for i in others[1:]]
    first += [functools.partial(turned, j) for j in others]
    pairs = [(a, b) for a in range(count - 1) for b in range(a, count - 1) if b > 0]
    rest = [functools.partial(update, others[a], others[b], k, x_ref, c_ref, g_ref) for a, b in pairs]
    share = -(-len(rest) // 3)
    return [first] + [rest[i * share:(i + 1) * share] for i in range(3)]


def boundary(k, x_ref, d_ref, c_ref, g_ref, w_ref):
    count = x_ref.shape[0] // BIG
    q = k + 1
    w = d_ref[...]
    split_to(w_ref, slice(None), w)
    x_ref[rows_of(k), rows_of(k)] = -w
    split_to(c_ref, rows_of(q), x_ref[rows_of(q), rows_of(k)])
    for r in range(0, BIG, SMALL):
        rows = pl.ds(pl.multiple_of(q * BIG + r, SMALL), SMALL)
        split_to(g_ref, rows, dot_nt(c_ref[rows, :], w_ref[...]))
        d_ref[r:r + SMALL, :] = x_ref[rows, rows_of(q)] - dot_nt(g_ref[rows, :], c_ref[rows_of(q), :])
    for i in others_of(k, count)[1:]:
        split_to(c_ref, rows_of(i), x_ref[rows_of(i), rows_of(k)])


def eliminate_blocks(start, stop, x_ref, ld_ref, d_ref, c_ref, g_ref, w_ref):
    count = x_ref.shape[0] // BIG

    def body(q, _):
        boundary(q - 1, x_ref, d_ref, c_ref, g_ref, w_ref)
        work = background(q - 1, count, x_ref, c_ref, g_ref, w_ref)
        for s in range(BIG // SMALL):
            small_step(s, d_ref, ld_ref)
            for unit in work[s]:
                unit()
        return 0

    lax.fori_loop(start, stop, body, 0)


def turned_halves(ref, u):
    split_at = u.shape[0]
    high, low = halves(u.T)
    ref[:, :split_at] = high
    ref[:, split_at:] = low


def blocks_of(size):
    return [slice(i, i + BIG) for i in range(0, size, BIG)]


def stacked(ref, part):
    depth = ref.shape[1] // 2 if part is not None else ref.shape[1]
    at = slice((part or 0) * depth, (part or 0) * depth + depth)
    return jnp.concatenate([ref[m, at, :] for m in range(ref.shape[0])], 0)


def own_columns(size, tile):
    return pl.ds(pl.multiple_of(tile * size, 128), size)


def column_of(row):
    here = lax.broadcasted_iota(jnp.int32, (128, 128), 0) == lax.broadcasted_iota(jnp.int32, (128, 128), 1)
    parts = [jnp.sum(jnp.where(here, row[:, i:i + 128], 0.0), 1, keepdims=True) for i in range(0, row.shape[1], 128)]
    return jnp.concatenate(parts, 0)


def split_scaled(ref, turned, scale):
    split_at = turned.shape[1]
    high, low = halves(turned * scale)
    ref[:, :split_at] = high
    ref[:, split_at:] = low


def first_kernel(numbers_ref, prior_in_ref, other_in_ref, rows_ref,
                 x_ref, d_ref, ld_ref, row_ref, c_ref, g_ref, w_ref, u_ref, col_ref, other_ref, prior_ref, in_sems):
    size = other_ref.shape[0]
    tile = lax.axis_index("tile")
    own_at, other_at = tile * size, (1 - tile) * size
    fetches = [pltpu.make_async_copy(other_in_ref.at[:, :size], other_ref, in_sems.at[0]),
               pltpu.make_async_copy(prior_in_ref, prior_ref, in_sems.at[1])]
    for fetch in fetches:
        fetch.start()
    weight_row, weight = numbers_ref[0:1, :], numbers_ref[0:1, 0:1]
    here = lax.broadcasted_iota(jnp.int32, (128, 128), 0) == lax.broadcasted_iota(jnp.int32, (128, 128), 1)

    def scale_at(i, square):
        row_ref[:, i:i + 128] = lax.rsqrt(weight_row * jnp.sum(jnp.where(here, square, 0.0), 0, keepdims=True))

    turned = stacked(rows_ref, None).T
    fetches[0].wait()
    for i in range(0, size, 128):
        scale_at(i, other_ref[i:i + 128, i:i + 128])
    col_ref[:size, :] = column_of(row_ref[:, :size])
    split_scaled(u_ref, turned, col_ref[:size, :])
    blocks = blocks_of(size)

    def corner(at, to):
        return other_ref[at, to] * (col_ref[at, :] * weight) * row_ref[:, to] + dot_nt(u_ref[at, :], u_ref[to, :])

    def build_other(at, to):
        x_ref[at, to] = corner(at, to)

    def build_low(at, to, base, start):
        low, far = slice(size + at.start, size + at.stop), slice(base + to.start, base + to.stop)
        cols = pl.ds(pl.multiple_of(start + to.start, 128), BIG)
        x_ref[low, far] = prior_ref[at, cols] * (col_ref[low, :] * weight) * row_ref[:, far]

    ld_ref[...] = jnp.zeros_like(ld_ref)
    d_ref[...] = corner(blocks[0], blocks[0])
    fetches[1].wait()
    for i in range(0, size, 128):
        scale_at(size + i, prior_ref[i:i + 128, pl.ds(pl.multiple_of(own_at + i, 128), 128)])
    col_ref[size:, :] = column_of(row_ref[:, size:])
    units = []
    for i, at in enumerate(blocks):
        units += [functools.partial(build_other, at, to) for j, to in enumerate(blocks) if 0 < i and j <= i]
        units += [functools.partial(build_low, at, to, 0, other_at) for to in blocks]
        units += [functools.partial(build_low, at, to, size, own_at) for j, to in enumerate(blocks) if j <= i]
    steps = BIG // SMALL
    for s in range(steps):
        small_step(s, d_ref, ld_ref)
        for unit in units[s::steps]:
            unit()
    eliminate_blocks(1, size // BIG, x_ref, ld_ref, d_ref, c_ref, g_ref, w_ref)


def upper_place(i, j, count):
    return i * count - i * (i - 1) // 2 + j - i


def second_kernel(x_in_ref, d_in_ref, ld_in_ref, rows_ref, row_ref, gain_ref,
                  send_out_ref, own_out_ref, x_ref, d_ref, c_ref, g_ref, w_ref, u_ref, left_ref, left_col_ref, ld_ref,
                  send_ref, own_ref, in_sem, out_sems):
    n = x_ref.shape[0]
    size = n // 2
    count = n // BIG
    half = size // BIG
    fetch = pltpu.make_async_copy(x_in_ref, x_ref, in_sem)
    fetch.start()
    d_ref[...] = d_in_ref[...]
    ld_ref[...] = ld_in_ref[...]
    turned_halves(u_ref, stacked(rows_ref, 0) * row_ref[:, size:])
    tile = lax.axis_index("tile")
    left_ref[:, :size] = row_ref[:, :size] * gain_ref[:, own_columns(size, 1 - tile)]
    left_ref[:, size:] = row_ref[:, size:] * gain_ref[:, own_columns(size, tile)]
    left_col_ref[...] = column_of(left_ref[...])
    fetch.wait()
    for i, at in enumerate(blocks_of(size)):
        for j, to in enumerate(blocks_of(size)):
            if j <= i:
                x_ref[size + at.start:size + at.stop, size + to.start:size + to.stop] += dot_nt(u_ref[at, :], u_ref[to, :])
    eliminate_blocks(half, count, x_ref, ld_ref, d_ref, c_ref, g_ref, w_ref)
    k = count - 1
    w = d_ref[...]
    split_to(w_ref, slice(None), w)

    def finish(a, b, value):
        rows, cols = slice(a * BIG, a * BIG + BIG), slice(b * BIG, b * BIG + BIG)
        value = -value * left_col_ref[rows, :] * left_ref[:, cols]
        if b < half:
            place = half * half + upper_place(a, b, half)
        else:
            place = a * half + b - half if a < half else upper_place(a - half, b - half, half)
        ref = send_ref if a < half else own_ref
        ref[place * BIG:place * BIG + BIG, :] = value

    total = ld_ref[...] - 2.0 * jnp.sum(jnp.log(row_ref[...]))
    send_ref[send_ref.shape[0] - REG[0]:, :] = jnp.concatenate([total] * (BIG // REG[1]), 1)
    finish(k, k, -w)
    for i in range(k):
        at = slice(i * BIG, i * BIG + BIG)
        c = x_ref[at, k * BIG:n]
        split_to(c_ref, at, c)
        g = dot_nt(c_ref[at, :], w_ref[...])
        split_to(g_ref, at, g)
        finish(i, k, g)
    for a in range(k):
        at = slice(a * BIG, a * BIG + BIG)
        for b in range(a, k):
            to = slice(b * BIG, b * BIG + BIG)
            finish(a, b, x_ref[at, to] - dot_nt(g_ref[at, :], c_ref[to, :]))
        if a == half - 1:
            send = pltpu.make_async_copy(send_ref, send_out_ref, out_sems.at[0])
            send.start()
    own = pltpu.make_async_copy(own_ref, own_out_ref.at[:own_ref.shape[0]], out_sems.at[1])
    own.start()
    send.wait()
    own.wait()


def states(n, rows):
    return [
        pltpu.VMEM((n, 2 * BIG), jnp.bfloat16),
        pltpu.VMEM((n, 2 * BIG), jnp.bfloat16),
        pltpu.VMEM((BIG, 2 * BIG), jnp.bfloat16),
        pltpu.VMEM((n // 2, 2 * rows), jnp.bfloat16),
    ]


def in_vmem(count):
    return [pl.BlockSpec(memory_space=pltpu.VMEM)] * count


def in_hbm(count):
    return [pl.BlockSpec(memory_space=pltpu.HBM)] * count


def first_half(numbers, prior, other, rows):
    size, n = prior.shape
    f32 = jnp.float32
    return pl.pallas_call(
        first_kernel,
        out_shape=(jax.ShapeDtypeStruct((n, n), f32), jax.ShapeDtypeStruct((BIG, BIG), f32), jax.ShapeDtypeStruct(REG, f32),
                   jax.ShapeDtypeStruct((1, n), f32)),
        in_specs=in_vmem(1) + in_hbm(2) + in_vmem(1),
        out_specs=tuple(in_vmem(4)),
        scratch_shapes=states(n, rows.shape[0] * rows.shape[1]) + [pltpu.VMEM((n, 1), f32), pltpu.VMEM((size, size), f32), pltpu.VMEM((size, n), f32), pltpu.SemaphoreType.DMA((2,))],
        compiler_params=pltpu.CompilerParams(vmem_limit_bytes=60 << 20),
        cost_estimate=pl.CostEstimate(flops=12 * n**3, bytes_accessed=8 * n * n, transcendentals=0),
    )(numbers, prior, other, rows)


def second_half(x, d, log_det, rows, row, gain):
    n = x.shape[0]
    size = n // 2
    f32 = jnp.float32
    half = size // BIG
    upper = half * (half + 1) // 2 * BIG
    send, own = (half * size + upper + REG[0], BIG), (upper, BIG)
    return pl.pallas_call(
        second_kernel,
        out_shape=(jax.ShapeDtypeStruct(send, f32),) * 2,
        in_specs=in_hbm(1) + in_vmem(5),
        out_specs=tuple(in_hbm(2)),
        scratch_shapes=[pltpu.VMEM((n, n), f32), pltpu.VMEM((BIG, BIG), f32)] + states(n, rows.shape[0] * rows.shape[1] // 2)
        + [pltpu.VMEM((1, n), f32), pltpu.VMEM((n, 1), f32), pltpu.VMEM(REG, f32), pltpu.VMEM(send, f32),
           pltpu.VMEM(own, f32), pltpu.SemaphoreType.DMA, pltpu.SemaphoreType.DMA((2,))],
        compiler_params=pltpu.CompilerParams(vmem_limit_bytes=58 << 20),
        cost_estimate=pl.CostEstimate(flops=12 * n**3, bytes_accessed=8 * n * n, transcendentals=0),
    )(x, d, log_det, rows, row, gain[None, :])


def last_kernel(numbers_ref, prior_in_ref, rows_ref, own_in_ref, sent_in_ref, got_in_ref,
                block_ref, coupling_ref, log_ref, prior_ref, own_ref, sent_ref, got_ref, block_buf, coupling_buf, u_ref, in_sems, sems):
    size, n = prior_ref.shape
    tile = lax.axis_index("tile")
    own_at = tile * size
    cross_at = size - own_at
    blocks = blocks_of(size)
    half = len(blocks)
    corner = half * size
    fetches = [pltpu.make_async_copy(own_in_ref.at[:own_ref.shape[0]], own_ref, in_sems.at[0]),
               pltpu.make_async_copy(sent_in_ref.at[:corner], sent_ref.at[:corner], in_sems.at[1]),
               pltpu.make_async_copy(got_in_ref.at[corner:], got_ref.at[corner:], in_sems.at[2]),
               pltpu.make_async_copy(sent_in_ref.at[sent_ref.shape[0] - REG[0]:], sent_ref.at[sent_ref.shape[0] - REG[0]:], in_sems.at[3])]
    for i, at in enumerate(blocks):
        part = slice(i * size, i * size + size)
        fetches.append(pltpu.make_async_copy(prior_in_ref.at[at], prior_ref.at[at], in_sems.at[4 + 2 * i]))
        fetches.append(pltpu.make_async_copy(got_in_ref.at[part], got_ref.at[part], in_sems.at[5 + 2 * i]))
    for fetch in fetches:
        fetch.start()

    def block(ref, place):
        return ref[place * BIG:place * BIG + BIG, :]

    def mirrored(ref, first, i, j):
        return block(ref, first + upper_place(i, j, half)) if i <= j else block(ref, first + upper_place(j, i, half)).T

    weight, have_block, got_block, have_coupling, got_coupling = [numbers_ref[i] for i in range(5)]
    turned_halves(u_ref, stacked(rows_ref, 1))
    copies = []
    for i, at in enumerate(blocks):
        for fetch in (fetches[:6] if i == 0 else fetches[4 + 2 * i:6 + 2 * i]):
            fetch.wait()
        for j, to in enumerate(blocks):
            for which in range(2):
                if which == 0:
                    have = mirrored(own_ref, 0, i, j)
                    got = mirrored(got_ref, half * half, i, j)
                    cols = pl.ds(pl.multiple_of(own_at + j * BIG, BIG), BIG)
                else:
                    have = block(sent_ref, j * half + i).T
                    got = block(got_ref, i * half + j)
                    cols = pl.ds(pl.multiple_of(cross_at + j * BIG, BIG), BIG)
                base = weight * prior_ref[at, cols]
                if which == 0:
                    base = base + dot_nt(u_ref[at, :], u_ref[to, :])
                block_buf[at, cols] = base - (have_block * have + got_block * got)
                coupling_buf[at, cols] = have_coupling * have + got_coupling * got
        for o, (buf, ref) in enumerate([(block_buf, block_ref), (coupling_buf, coupling_ref)]):
            copy = pltpu.make_async_copy(buf.at[at], ref.at[at], sems.at[2 * i + o])
            copy.start()
            copies.append(copy)
    foot = slice(got_ref.shape[0] - REG[0], got_ref.shape[0])
    log_ref[...] = jnp.where(tile == 0, sent_ref[foot, :REG[1]], got_ref[foot, :REG[1]]) / n
    for copy in copies:
        copy.wait()


def outputs(numbers, prior, rows, own, send, got):
    size, n = prior.shape
    f32 = jnp.float32
    count = size // BIG
    return pl.pallas_call(
        last_kernel,
        out_shape=(jax.ShapeDtypeStruct((size, n), f32),) * 2 + (jax.ShapeDtypeStruct(REG, f32),),
        in_specs=[pl.BlockSpec(memory_space=pltpu.SMEM)] + in_hbm(1) + in_vmem(1) + in_hbm(3),
        out_specs=tuple(in_hbm(2) + in_vmem(1)),
        scratch_shapes=[pltpu.VMEM((size, n), f32), pltpu.VMEM((count * (count + 1) // 2 * BIG, BIG), f32), pltpu.VMEM(send.shape, f32), pltpu.VMEM(got.shape, f32)] + [pltpu.VMEM((size, n), f32)] * 2
        + [pltpu.VMEM((size, rows.shape[0] * rows.shape[1]), jnp.bfloat16), pltpu.SemaphoreType.DMA((2 * count + 4,)),
           pltpu.SemaphoreType.DMA((2 * count,))],
        compiler_params=pltpu.CompilerParams(vmem_limit_bytes=60 << 20),
        cost_estimate=pl.CostEstimate(flops=6 * size * size * n, bytes_accessed=20 * size * n, transcendentals=0),
    )(numbers, prior, rows, own, send, got)


def order_kernel(step_ref, value_ref, weight_ref, first_ref, rest_ref):
    parts = first_ref.shape[0] - 1
    tile = lax.axis_index("tile")
    root = jnp.sqrt(weight_ref[...]).T
    for k in range(value_ref.shape[0]):
        step = step_ref[k]
        part, odd = lax.shift_right_logical(step, 1), (step & 1) == 1
        rows = value_ref[k] * root[:, k:k + 1]
        before = jnp.where(part == 0, parts - 1, part - 1)
        at_zero, at_one = part, before
        first_ref[jnp.where(odd, parts, jnp.where(tile == 0, at_one, at_zero))] = rows
        rest_ref[2 * jnp.where(odd | (tile == 0), at_zero, at_one) + (step & 1)] = rows


def by_step(values, weights, steps, parts):
    depth, size = values.shape[1:]
    return pl.pallas_call(
        order_kernel,
        out_shape=(jax.ShapeDtypeStruct((parts + 1, depth, size), jnp.float32), jax.ShapeDtypeStruct((2 * parts, depth, size), jnp.float32)),
        in_specs=[
            pl.BlockSpec(memory_space=pltpu.SMEM),
            pl.BlockSpec(memory_space=pltpu.VMEM),
            pl.BlockSpec(memory_space=pltpu.VMEM),
        ],
        out_specs=tuple(in_vmem(2)),
        compiler_params=pltpu.CompilerParams(vmem_limit_bytes=40 << 20),
    )(steps, values, weights)


def exchange_kernel(time_ref, rho_ref, first_ref, prior_ref, rows_ref, other_ref, numbers_ref, mine_ref, next_ref, send_sems, recv_sems):
    parts = rows_ref.shape[0]
    size = prior_ref.shape[0]
    me, tile = lax.axis_index("tm"), lax.axis_index("tile")
    there = 1 - tile
    after, before = lax.rem(me + 1, parts), lax.rem(me + parts - 1, parts)
    mesh = pl.DeviceIdType.MESH
    barrier = pltpu.get_barrier_semaphore()
    for i in range(parts):
        pl.semaphore_signal(barrier, inc=1, device_id=(lax.rem(me + i, parts), there), device_id_type=mesh)
    pl.semaphore_signal(barrier, inc=1, device_id=(after, tile), device_id_type=mesh)
    mine_ref[0:1, :] = jnp.full((1, REG[1]), time_ref[0], jnp.float32)
    mine_ref[1:2, :] = jnp.full((1, REG[1]), rho_ref[0], jnp.float32)
    mine_ref[2:, :] = jnp.zeros((REG[0] - 2, REG[1]), jnp.float32)
    pl.semaphore_wait(barrier, parts + 1)

    def rows_copy(i, slot):
        to = lax.rem(me + i, parts)
        return pltpu.make_async_remote_copy(
            src_ref=first_ref.at[to], dst_ref=rows_ref.at[slot], send_sem=send_sems.at[i],
            recv_sem=recv_sems.at[slot], device_id=(to, there), device_id_type=mesh)

    scalars = pltpu.make_async_remote_copy(
        src_ref=mine_ref, dst_ref=next_ref, send_sem=send_sems.at[parts], recv_sem=recv_sems.at[parts],
        device_id=(before, tile), device_id_type=mesh)
    prior = pltpu.make_async_remote_copy(
        src_ref=prior_ref.at[:, own_columns(size, tile)], dst_ref=other_ref.at[:, :size], send_sem=send_sems.at[parts + 1],
        recv_sem=recv_sems.at[parts + 1], device_id=(me, there), device_id_type=mesh)
    scalars.start()
    for i in range(parts - 1, -1, -1):
        rows_copy(i, me).start()
    prior.start()
    scalars.wait()
    last = me == parts - 1
    own, following = mine_ref[...], next_ref[...]
    row = lax.broadcasted_iota(jnp.int32, REG, 0)
    chosen = jnp.where(tile == 0, own, jnp.where(last, 1.0, following))
    numbers_ref[...] = jnp.where(row == 0, chosen, jnp.where(last, 0.0, following))
    for i in range(parts):
        rows_copy(i, me).wait_send()
    for i in range(parts):
        rows_copy(i, lax.rem(me + i, parts)).wait_recv()
    prior.wait()


def exchange(time_diag, rho, first, prior):
    parts = first.shape[0] - 1
    size = prior.shape[0]
    f32 = jnp.float32
    return pl.pallas_call(
        exchange_kernel,
        out_shape=(jax.ShapeDtypeStruct((parts,) + first.shape[1:], f32), jax.ShapeDtypeStruct(prior.shape, f32), jax.ShapeDtypeStruct(REG, f32)),
        in_specs=[pl.BlockSpec(memory_space=pltpu.SMEM)] * 2 + in_vmem(1) + in_hbm(1),
        out_specs=tuple(in_vmem(1) + in_hbm(1) + in_vmem(1)),
        scratch_shapes=[pltpu.VMEM(REG, f32)] * 2 + [pltpu.SemaphoreType.DMA((parts + 2,))] * 2,
        compiler_params=pltpu.CompilerParams(collective_id=0, has_side_effects=True, vmem_limit_bytes=58 << 20),
        cost_estimate=pl.CostEstimate(flops=0, bytes_accessed=4 * size * size, transcendentals=0),
    )(time_diag, rho, first, prior)


def on_device(prior_space, node_gain, time_diag, rho, obs_values, obs_weight, obs_step):
    size = prior_space.shape[0]
    parts = lax.axis_size("tm")
    tile = lax.axis_index("tile")
    first = tile == 0

    def chosen(a, b):
        return jnp.where(first, a, b)

    sent, rest = by_step(obs_values[0], obs_weight[0], obs_step[0, 0], parts)
    rows_other, prior_other, numbers = exchange(time_diag, rho, sent, prior_space)
    rest, rows_other = lax.optimization_barrier((rest, rows_other))
    rest = lax.all_to_all(rest.reshape(parts, -1, size), "tm", split_axis=0, concat_axis=0, tiled=True)

    x, d, log_det, row = first_half(numbers, prior_space, prior_other, rows_other)
    send, own = second_half(x, d, log_det, rest, row, node_gain)
    got = lax.ppermute(send, "tile", [(0, 1), (1, 0)])

    now, following, across = rho[1] * rho[1], numbers[1, 0] * numbers[1, 0], -(rho[0] * rho[1])
    factors = jnp.stack([time_diag[1], chosen(now, following), chosen(following, now), chosen(across, 0.0), chosen(0.0, across)])
    block, coupling, log_det = outputs(factors, prior_space, rest, own, send, got)
    return block[None], coupling[None], log_det[0, :1]


def solution(mesh):
    in_specs = (
        P("tile", None),
        P(),
        P("tm"),
        P("tm"),
        P("tile", "tm", None, None),
        P("tile", "tm", None),
        P("tile", "tm", None),
    )
    out_specs = (P("tm", "tile", None), P("tm", "tile", None), P("tm"))
    return jax.shard_map(
        on_device, mesh=mesh, in_specs=in_specs, out_specs=out_specs, check_vma=False
    )
```

```python
import functools
import jax, jax.numpy as jnp
from jax import lax
from jax.experimental import pallas as pl
from jax.experimental.pallas import tpu as pltpu
from jax.sharding import PartitionSpec as P

REG = (8, 128)
BIG, SMALL = 256, 64


def along(x, j):
    return jnp.broadcast_to(x[:, j:j + 1], REG)


def down(x, i):
    return jnp.take_along_axis(x, jnp.full(REG, i, jnp.int32), axis=0)


def halves(x):
    high = x.astype(jnp.bfloat16)
    return high, (x - high.astype(jnp.float32)).astype(jnp.bfloat16)


def dot_nn(a, b):
    ah, al = halves(a)
    bh, bl = halves(b)
    return jnp.dot(jnp.concatenate([ah, al, ah], 1), jnp.concatenate([bh, bh, bl], 0), preferred_element_type=jnp.float32)


def pair_inverse(a, b, d):
    det = a * d - b * b
    r = 1.0 / det
    return d * r, -(b * r), a * r, det


def inverse_of_four(s):
    a, b, d, det1 = pair_inverse(s[0, 0], s[1, 0], s[1, 1])
    q = [[s[2, 0], s[2, 1]], [s[3, 0], s[3, 1]]]
    m = [[q[i][0] * a + q[i][1] * b, q[i][0] * b + q[i][1] * d] for i in range(2)]
    u = s[2, 2] - (m[0][0] * q[0][0] + m[0][1] * q[0][1])
    v = s[3, 2] - (m[1][0] * q[0][0] + m[1][1] * q[0][1])
    w = s[3, 3] - (m[1][0] * q[1][0] + m[1][1] * q[1][1])
    u, v, w, det2 = pair_inverse(u, v, w)
    low = [[u * m[0][j] + v * m[1][j] for j in range(2)], [v * m[0][j] + w * m[1][j] for j in range(2)]]
    w00 = a + (m[0][0] * low[0][0] + m[1][0] * low[1][0])
    w01 = b + (m[0][0] * low[0][1] + m[1][0] * low[1][1])
    w11 = d + (m[0][1] * low[0][1] + m[1][1] * low[1][1])
    inverse = [[w00, w01, -low[0][0], -low[1][0]],
               [w01, w11, -low[0][1], -low[1][1]],
               [-low[0][0], -low[0][1], u, v],
               [-low[1][0], -low[1][1], v, w]]
    return inverse, det1, det2


def eliminate(tiles, log_det, offset):
    lane = lax.broadcasted_iota(jnp.int32, REG, 1) - offset
    sub = lax.broadcasted_iota(jnp.int32, REG, 0)
    for home in range(len(tiles)):
        p = 8 * home
        cols = [[along(t, offset + p + j) for t in tiles] for j in range(8)]
        c = [cols[j][home] for j in range(8)]
        head, det1, det2 = inverse_of_four({(i, j): down(c[j], i) for j in range(4) for i in range(j, 4)})
        slope = [weighted([head[i][j] for i in range(4)], c[:4]) for j in range(4)]
        rest = [c[j] - weighted([down(c[j], i) for i in range(4)], slope) for j in range(4, 8)]
        foot, det3, det4 = inverse_of_four({(i, j): down(rest[j], i + 4) for j in range(4) for i in range(j, 4)})
        log_det = log_det + ((jnp.log(det1) + jnp.log(det2)) + (jnp.log(det3) + jnp.log(det4)))
        here = (lane >= p) & (lane < p + 8)
        rows = jnp.where(here, jnp.where(lane == p + sub, 1.0, 0.0), tiles[home])
        top = [down(rows, i) for i in range(4)]
        upper = [weighted(head[i], top) for i in range(4)]
        rows = rows - weighted(c[:4], upper)
        low = [down(rows, i) for i in range(4, 8)]
        lower = [weighted(foot[i], low) for i in range(4)]
        upper = [upper[i] - weighted([down(slope[i], j) for j in range(4, 8)], lower) for i in range(4)]
        out = upper + lower
        new = []
        for t, tile in enumerate(tiles):
            if t == home:
                kept = out[0]
                for i in range(1, 8):
                    kept = jnp.where(sub == i, out[i], kept)
            else:
                kept = jnp.where(here, 0.0, tile)
                kept = kept - (weighted([cols[j][t] for j in range(4)], out[:4]) + weighted([cols[j][t] for j in range(4, 8)], out[4:]))
            new.append(kept)
        tiles = new
    return tiles, log_det


def weighted(a, b):
    return (a[0] * b[0] + a[1] * b[1]) + (a[2] * b[2] + a[3] * b[3])


def small_step(s, d_ref, ld_ref):
    half, offset = s // 2, (s % 2) * SMALL
    mine, others = slice(128 * half, 128 * half + 128), slice(128 * (1 - half), 128 * (1 - half) + 128)
    at = slice(SMALL * s, SMALL * s + SMALL)
    tiles = [d_ref[SMALL * s + 8 * t:SMALL * s + 8 * t + 8, mine] for t in range(SMALL // 8)]
    tiles, ld = eliminate(tiles, ld_ref[...], offset)
    ld_ref[...] = ld
    panel = jnp.concatenate(tiles, 0)
    gap = jnp.zeros((SMALL, 128), jnp.float32)

    def inside(rows):
        lane = lax.broadcasted_iota(jnp.int32, (rows, 128), 1)
        return (lane >= offset) & (lane < offset + SMALL)

    def padded(x):
        return jnp.concatenate([x, gap] if offset == 0 else [gap, x], 0)

    across = dot_nn(jnp.where(inside(SMALL), panel, 0.0), padded(d_ref[at, others]))
    d_ref[at, :] = jnp.concatenate([panel, across] if half == 0 else [across, panel], 1)
    left = {}
    for r in [(s + 1 + i) % 4 for i in range(3)]:
        rows = slice(SMALL * r, SMALL * r + SMALL)
        own = d_ref[rows, mine]
        left[r] = jnp.where(inside(SMALL), own, 0.0)
        if offset:
            d_ref[rows, others] -= dot_nn(left[r], padded(across))
            d_ref[rows, mine] = jnp.where(inside(SMALL), 0.0, own) - dot_nn(left[r], padded(panel))
        else:
            d_ref[rows, mine] = jnp.where(inside(SMALL), 0.0, own) - dot_nn(left[r], padded(panel))
            d_ref[rows, others] -= dot_nn(left[r], padded(across))


def dot_nt(a, b):
    k = a.shape[1] // 2
    left = jnp.concatenate([a, a[:, :k]], 1)
    right = jnp.concatenate([b[:, :k], b[:, :k], b[:, k:]], 1)
    return lax.dot_general(left, right, (((1,), (1,)), ((), ())), preferred_element_type=jnp.float32)


def rows_of(i):
    return pl.ds(pl.multiple_of(i * BIG, BIG), BIG)


def split_to(ref, at, x):
    high, low = halves(x)
    ref[at, :BIG] = high
    ref[at, BIG:] = low


def others_of(k, count):
    return [lax.rem(k + 1 + i, count) for i in range(count - 1)]


def gain(i, k, x_ref, c_ref, g_ref, w_ref):
    g = dot_nt(c_ref[rows_of(i), :], w_ref[...])
    split_to(g_ref, rows_of(i), g)
    x_ref[rows_of(i), rows_of(k)] = g


def update(u, v, k, x_ref, c_ref, g_ref):
    low, high = jnp.minimum(u, v), jnp.maximum(u, v)
    r, c = jnp.where(low < k, low, high), jnp.where(low < k, high, low)
    x_ref[rows_of(r), rows_of(c)] -= dot_nt(g_ref[rows_of(r), :], c_ref[rows_of(c), :])


def background(k, count, x_ref, c_ref, g_ref, w_ref):
    others = others_of(k, count)

    def turned(j):
        x_ref[rows_of(k), rows_of(j)] = dot_nt(w_ref[...], c_ref[rows_of(j), :])

    first = [functools.partial(gain, i, k, x_ref, c_ref, g_ref, w_ref) for i in others[1:]]
    first += [functools.partial(turned, j) for j in others]
    pairs = [(a, b) for a in range(count - 1) for b in range(a, count - 1) if b > 0]
    rest = [functools.partial(update, others[a], others[b], k, x_ref, c_ref, g_ref) for a, b in pairs]
    share = -(-len(rest) // 3)
    return [first] + [rest[i * share:(i + 1) * share] for i in range(3)]


def boundary(k, x_ref, d_ref, c_ref, g_ref, w_ref):
    count = x_ref.shape[0] // BIG
    q = k + 1
    w = d_ref[...]
    split_to(w_ref, slice(None), w)
    x_ref[rows_of(k), rows_of(k)] = -w
    split_to(c_ref, rows_of(q), x_ref[rows_of(q), rows_of(k)])
    for r in range(0, BIG, SMALL):
        rows = pl.ds(pl.multiple_of(q * BIG + r, SMALL), SMALL)
        split_to(g_ref, rows, dot_nt(c_ref[rows, :], w_ref[...]))
        d_ref[r:r + SMALL, :] = x_ref[rows, rows_of(q)] - dot_nt(g_ref[rows, :], c_ref[rows_of(q), :])
    for i in others_of(k, count)[1:]:
        split_to(c_ref, rows_of(i), x_ref[rows_of(i), rows_of(k)])


def eliminate_blocks(start, stop, x_ref, ld_ref, d_ref, c_ref, g_ref, w_ref):
    count = x_ref.shape[0] // BIG

    def body(q, _):
        boundary(q - 1, x_ref, d_ref, c_ref, g_ref, w_ref)
        work = background(q - 1, count, x_ref, c_ref, g_ref, w_ref)
        for s in range(BIG // SMALL):
            small_step(s, d_ref, ld_ref)
            for unit in work[s]:
                unit()
        return 0

    lax.fori_loop(start, stop, body, 0)


def turned_halves(ref, u):
    split_at = u.shape[0]
    high, low = halves(u.T)
    ref[:, :split_at] = high
    ref[:, split_at:] = low


def blocks_of(size):
    return [slice(i, i + BIG) for i in range(0, size, BIG)]


def stacked(ref, part):
    depth = ref.shape[1] // 2 if part is not None else ref.shape[1]
    at = slice((part or 0) * depth, (part or 0) * depth + depth)
    return jnp.concatenate([ref[m, at, :] for m in range(ref.shape[0])], 0)


def own_columns(size, tile):
    return pl.ds(pl.multiple_of(tile * size, 128), size)


def column_of(row):
    here = lax.broadcasted_iota(jnp.int32, (128, 128), 0) == lax.broadcasted_iota(jnp.int32, (128, 128), 1)
    parts = [jnp.sum(jnp.where(here, row[:, i:i + 128], 0.0), 1, keepdims=True) for i in range(0, row.shape[1], 128)]
    return jnp.concatenate(parts, 0)


def split_scaled(ref, turned, scale):
    split_at = turned.shape[1]
    high, low = halves(turned * scale)
    ref[:, :split_at] = high
    ref[:, split_at:] = low


def first_kernel(numbers_ref, prior_in_ref, other_in_ref, rows_ref,
                 x_ref, d_ref, ld_ref, row_ref, c_ref, g_ref, w_ref, u_ref, col_ref, other_ref, prior_ref, in_sems):
    size = other_ref.shape[0]
    tile = lax.axis_index("tile")
    own_at, other_at = tile * size, (1 - tile) * size
    fetches = [pltpu.make_async_copy(other_in_ref.at[:, :size], other_ref, in_sems.at[0]),
               pltpu.make_async_copy(prior_in_ref, prior_ref, in_sems.at[1])]
    for fetch in fetches:
        fetch.start()
    weight_row, weight = numbers_ref[0:1, :], numbers_ref[0:1, 0:1]
    here = lax.broadcasted_iota(jnp.int32, (128, 128), 0) == lax.broadcasted_iota(jnp.int32, (128, 128), 1)

    def scale_at(i, square):
        row_ref[:, i:i + 128] = lax.rsqrt(weight_row * jnp.sum(jnp.where(here, square, 0.0), 0, keepdims=True))

    turned = stacked(rows_ref, None).T
    fetches[0].wait()
    for i in range(0, size, 128):
        scale_at(i, other_ref[i:i + 128, i:i + 128])
    col_ref[:size, :] = column_of(row_ref[:, :size])
    split_scaled(u_ref, turned, col_ref[:size, :])
    blocks = blocks_of(size)

    def corner(at, to):
        return other_ref[at, to] * (col_ref[at, :] * weight) * row_ref[:, to] + dot_nt(u_ref[at, :], u_ref[to, :])

    def build_other(at, to):
        x_ref[at, to] = corner(at, to)

    def build_low(at, to, base, start):
        low, far = slice(size + at.start, size + at.stop), slice(base + to.start, base + to.stop)
        cols = pl.ds(pl.multiple_of(start + to.start, 128), BIG)
        x_ref[low, far] = prior_ref[at, cols] * (col_ref[low, :] * weight) * row_ref[:, far]

    ld_ref[...] = jnp.zeros_like(ld_ref)
    d_ref[...] = corner(blocks[0], blocks[0])
    fetches[1].wait()
    for i in range(0, size, 128):
        scale_at(size + i, prior_ref[i:i + 128, pl.ds(pl.multiple_of(own_at + i, 128), 128)])
    col_ref[size:, :] = column_of(row_ref[:, size:])
    units = []
    for i, at in enumerate(blocks):
        units += [functools.partial(build_other, at, to) for j, to in enumerate(blocks) if 0 < i and j <= i]
        units += [functools.partial(build_low, at, to, 0, other_at) for to in blocks]
        units += [functools.partial(build_low, at, to, size, own_at) for j, to in enumerate(blocks) if j <= i]
    steps = BIG // SMALL
    for s in range(steps):
        small_step(s, d_ref, ld_ref)
        for unit in units[s::steps]:
            unit()
    eliminate_blocks(1, size // BIG, x_ref, ld_ref, d_ref, c_ref, g_ref, w_ref)


def upper_place(i, j, count):
    return i * count - i * (i - 1) // 2 + j - i


def second_kernel(x_in_ref, d_in_ref, ld_in_ref, rows_ref, row_ref, gain_ref,
                  send_out_ref, own_out_ref, x_ref, d_ref, c_ref, g_ref, w_ref, u_ref, left_ref, left_col_ref, ld_ref,
                  send_ref, own_ref, in_sem, out_sems):
    n = x_ref.shape[0]
    size = n // 2
    count = n // BIG
    half = size // BIG
    fetch = pltpu.make_async_copy(x_in_ref, x_ref, in_sem)
    fetch.start()
    d_ref[...] = d_in_ref[...]
    ld_ref[...] = ld_in_ref[...]
    turned_halves(u_ref, stacked(rows_ref, 0) * row_ref[:, size:])
    tile = lax.axis_index("tile")
    left_ref[:, :size] = row_ref[:, :size] * gain_ref[:, own_columns(size, 1 - tile)]
    left_ref[:, size:] = row_ref[:, size:] * gain_ref[:, own_columns(size, tile)]
    left_col_ref[...] = column_of(left_ref[...])
    fetch.wait()
    for i, at in enumerate(blocks_of(size)):
        for j, to in enumerate(blocks_of(size)):
            if j <= i:
                x_ref[size + at.start:size + at.stop, size + to.start:size + to.stop] += dot_nt(u_ref[at, :], u_ref[to, :])
    eliminate_blocks(half, count, x_ref, ld_ref, d_ref, c_ref, g_ref, w_ref)
    k = count - 1
    w = d_ref[...]
    split_to(w_ref, slice(None), w)

    def finish(a, b, value):
        rows, cols = slice(a * BIG, a * BIG + BIG), slice(b * BIG, b * BIG + BIG)
        value = -value * left_col_ref[rows, :] * left_ref[:, cols]
        if b < half:
            place = half * half + upper_place(a, b, half)
        else:
            place = a * half + b - half if a < half else upper_place(a - half, b - half, half)
        ref = send_ref if a < half else own_ref
        ref[place * BIG:place * BIG + BIG, :] = value

    total = ld_ref[...] - 2.0 * jnp.sum(jnp.log(row_ref[...]))
    send_ref[send_ref.shape[0] - REG[0]:, :] = jnp.concatenate([total] * (BIG // REG[1]), 1)
    finish(k, k, -w)
    for i in range(k):
        at = slice(i * BIG, i * BIG + BIG)
        c = x_ref[at, k * BIG:n]
        split_to(c_ref, at, c)
        g = dot_nt(c_ref[at, :], w_ref[...])
        split_to(g_ref, at, g)
        finish(i, k, g)
    for a in range(k):
        at = slice(a * BIG, a * BIG + BIG)
        for b in range(a, k):
            to = slice(b * BIG, b * BIG + BIG)
            finish(a, b, x_ref[at, to] - dot_nt(g_ref[at, :], c_ref[to, :]))
        if a == half - 1:
            send = pltpu.make_async_copy(send_ref, send_out_ref, out_sems.at[0])
            send.start()
    own = pltpu.make_async_copy(own_ref, own_out_ref.at[:own_ref.shape[0]], out_sems.at[1])
    own.start()
    send.wait()
    own.wait()


def states(n, rows):
    return [
        pltpu.VMEM((n, 2 * BIG), jnp.bfloat16),
        pltpu.VMEM((n, 2 * BIG), jnp.bfloat16),
        pltpu.VMEM((BIG, 2 * BIG), jnp.bfloat16),
        pltpu.VMEM((n // 2, 2 * rows), jnp.bfloat16),
    ]


def in_vmem(count):
    return [pl.BlockSpec(memory_space=pltpu.VMEM)] * count


def in_hbm(count):
    return [pl.BlockSpec(memory_space=pltpu.HBM)] * count


def first_half(numbers, prior, other, rows):
    size, n = prior.shape
    f32 = jnp.float32
    return pl.pallas_call(
        first_kernel,
        out_shape=(jax.ShapeDtypeStruct((n, n), f32), jax.ShapeDtypeStruct((BIG, BIG), f32), jax.ShapeDtypeStruct(REG, f32),
                   jax.ShapeDtypeStruct((1, n), f32)),
        in_specs=in_vmem(1) + in_hbm(2) + in_vmem(1),
        out_specs=tuple(in_vmem(4)),
        scratch_shapes=states(n, rows.shape[0] * rows.shape[1]) + [pltpu.VMEM((n, 1), f32), pltpu.VMEM((size, size), f32), pltpu.VMEM((size, n), f32), pltpu.SemaphoreType.DMA((2,))],
        compiler_params=pltpu.CompilerParams(vmem_limit_bytes=52 << 20),
        cost_estimate=pl.CostEstimate(flops=12 * n**3, bytes_accessed=8 * n * n, transcendentals=0),
    )(numbers, prior, other, rows)


def second_half(x, d, log_det, rows, row, gain):
    n = x.shape[0]
    size = n // 2
    f32 = jnp.float32
    half = size // BIG
    upper = half * (half + 1) // 2 * BIG
    send, own = (half * size + upper + REG[0], BIG), (upper, BIG)
    return pl.pallas_call(
        second_kernel,
        out_shape=(jax.ShapeDtypeStruct(send, f32),) * 2,
        in_specs=in_hbm(1) + in_vmem(5),
        out_specs=tuple(in_hbm(2)),
        scratch_shapes=[pltpu.VMEM((n, n), f32), pltpu.VMEM((BIG, BIG), f32)] + states(n, rows.shape[0] * rows.shape[1] // 2)
        + [pltpu.VMEM((1, n), f32), pltpu.VMEM((n, 1), f32), pltpu.VMEM(REG, f32), pltpu.VMEM(send, f32),
           pltpu.VMEM(own, f32), pltpu.SemaphoreType.DMA, pltpu.SemaphoreType.DMA((2,))],
        compiler_params=pltpu.CompilerParams(vmem_limit_bytes=52 << 20),
        cost_estimate=pl.CostEstimate(flops=12 * n**3, bytes_accessed=8 * n * n, transcendentals=0),
    )(x, d, log_det, rows, row, gain[None, :])


def last_kernel(numbers_ref, prior_in_ref, rows_ref, own_in_ref, sent_in_ref, got_in_ref,
                block_ref, coupling_ref, log_ref, prior_ref, own_ref, sent_ref, got_ref, block_buf, coupling_buf, u_ref, in_sems, sems):
    size, n = prior_ref.shape
    tile = lax.axis_index("tile")
    own_at = tile * size
    cross_at = size - own_at
    blocks = blocks_of(size)
    half = len(blocks)
    corner = half * size
    fetches = [pltpu.make_async_copy(own_in_ref.at[:own_ref.shape[0]], own_ref, in_sems.at[0]),
               pltpu.make_async_copy(sent_in_ref.at[:corner], sent_ref.at[:corner], in_sems.at[1]),
               pltpu.make_async_copy(got_in_ref.at[corner:], got_ref.at[corner:], in_sems.at[2]),
               pltpu.make_async_copy(sent_in_ref.at[sent_ref.shape[0] - REG[0]:], sent_ref.at[sent_ref.shape[0] - REG[0]:], in_sems.at[3])]
    for i, at in enumerate(blocks):
        part = slice(i * size, i * size + size)
        fetches.append(pltpu.make_async_copy(prior_in_ref.at[at], prior_ref.at[at], in_sems.at[4 + 2 * i]))
        fetches.append(pltpu.make_async_copy(got_in_ref.at[part], got_ref.at[part], in_sems.at[5 + 2 * i]))
    for fetch in fetches:
        fetch.start()

    def block(ref, place):
        return ref[place * BIG:place * BIG + BIG, :]

    def mirrored(ref, first, i, j):
        return block(ref, first + upper_place(i, j, half)) if i <= j else block(ref, first + upper_place(j, i, half)).T

    weight, have_block, got_block, have_coupling, got_coupling = [numbers_ref[i] for i in range(5)]
    turned_halves(u_ref, stacked(rows_ref, 1))
    copies = []
    for i, at in enumerate(blocks):
        for fetch in (fetches[:6] if i == 0 else fetches[4 + 2 * i:6 + 2 * i]):
            fetch.wait()
        for j, to in enumerate(blocks):
            for which in range(2):
                if which == 0:
                    have = mirrored(own_ref, 0, i, j)
                    got = mirrored(got_ref, half * half, i, j)
                    cols = pl.ds(pl.multiple_of(own_at + j * BIG, BIG), BIG)
                else:
                    have = block(sent_ref, j * half + i).T
                    got = block(got_ref, i * half + j)
                    cols = pl.ds(pl.multiple_of(cross_at + j * BIG, BIG), BIG)
                base = weight * prior_ref[at, cols]
                if which == 0:
                    base = base + dot_nt(u_ref[at, :], u_ref[to, :])
                block_buf[at, cols] = base - (have_block * have + got_block * got)
                coupling_buf[at, cols] = have_coupling * have + got_coupling * got
        for o, (buf, ref) in enumerate([(block_buf, block_ref), (coupling_buf, coupling_ref)]):
            copy = pltpu.make_async_copy(buf.at[at], ref.at[at], sems.at[2 * i + o])
            copy.start()
            copies.append(copy)
    foot = slice(got_ref.shape[0] - REG[0], got_ref.shape[0])
    log_ref[...] = jnp.where(tile == 0, sent_ref[foot, :REG[1]], got_ref[foot, :REG[1]]) / n
    for copy in copies:
        copy.wait()


def outputs(numbers, prior, rows, own, send, got):
    size, n = prior.shape
    f32 = jnp.float32
    count = size // BIG
    return pl.pallas_call(
        last_kernel,
        out_shape=(jax.ShapeDtypeStruct((size, n), f32),) * 2 + (jax.ShapeDtypeStruct(REG, f32),),
        in_specs=[pl.BlockSpec(memory_space=pltpu.SMEM)] + in_hbm(1) + in_vmem(1) + in_hbm(3),
        out_specs=tuple(in_hbm(2) + in_vmem(1)),
        scratch_shapes=[pltpu.VMEM((size, n), f32), pltpu.VMEM((count * (count + 1) // 2 * BIG, BIG), f32), pltpu.VMEM(send.shape, f32), pltpu.VMEM(got.shape, f32)] + [pltpu.VMEM((size, n), f32)] * 2
        + [pltpu.VMEM((size, rows.shape[0] * rows.shape[1]), jnp.bfloat16), pltpu.SemaphoreType.DMA((2 * count + 4,)),
           pltpu.SemaphoreType.DMA((2 * count,))],
        compiler_params=pltpu.CompilerParams(vmem_limit_bytes=52 << 20),
        cost_estimate=pl.CostEstimate(flops=6 * size * size * n, bytes_accessed=20 * size * n, transcendentals=0),
    )(numbers, prior, rows, own, send, got)


def order_kernel(step_ref, value_ref, weight_ref, first_ref, rest_ref):
    parts = first_ref.shape[0] - 1
    tile = lax.axis_index("tile")
    root = jnp.sqrt(weight_ref[...]).T
    for k in range(value_ref.shape[0]):
        step = step_ref[k]
        part, odd = lax.shift_right_logical(step, 1), (step & 1) == 1
        rows = value_ref[k] * root[:, k:k + 1]
        before = jnp.where(part == 0, parts - 1, part - 1)
        at_zero, at_one = part, before
        first_ref[jnp.where(odd, parts, jnp.where(tile == 0, at_one, at_zero))] = rows
        rest_ref[2 * jnp.where(odd | (tile == 0), at_zero, at_one) + (step & 1)] = rows


def by_step(values, weights, steps, parts):
    depth, size = values.shape[1:]
    return pl.pallas_call(
        order_kernel,
        out_shape=(jax.ShapeDtypeStruct((parts + 1, depth, size), jnp.float32), jax.ShapeDtypeStruct((2 * parts, depth, size), jnp.float32)),
        in_specs=[
            pl.BlockSpec(memory_space=pltpu.SMEM),
            pl.BlockSpec(memory_space=pltpu.VMEM),
            pl.BlockSpec(memory_space=pltpu.VMEM),
        ],
        out_specs=tuple(in_vmem(2)),
        compiler_params=pltpu.CompilerParams(vmem_limit_bytes=40 << 20),
    )(steps, values, weights)


def exchange_kernel(time_ref, rho_ref, first_ref, prior_ref, rows_ref, other_ref, numbers_ref, mine_ref, next_ref, send_sems, recv_sems):
    parts = rows_ref.shape[0]
    size = prior_ref.shape[0]
    me, tile = lax.axis_index("tm"), lax.axis_index("tile")
    there = 1 - tile
    after, before = lax.rem(me + 1, parts), lax.rem(me + parts - 1, parts)
    mesh = pl.DeviceIdType.MESH
    barrier = pltpu.get_barrier_semaphore()
    for i in range(parts):
        pl.semaphore_signal(barrier, inc=1, device_id=(lax.rem(me + i, parts), there), device_id_type=mesh)
    pl.semaphore_signal(barrier, inc=1, device_id=(after, tile), device_id_type=mesh)
    mine_ref[0:1, :] = jnp.full((1, REG[1]), time_ref[0], jnp.float32)
    mine_ref[1:2, :] = jnp.full((1, REG[1]), rho_ref[0], jnp.float32)
    mine_ref[2:, :] = jnp.zeros((REG[0] - 2, REG[1]), jnp.float32)
    pl.semaphore_wait(barrier, parts + 1)

    def rows_copy(i, slot):
        to = lax.rem(me + i, parts)
        return pltpu.make_async_remote_copy(
            src_ref=first_ref.at[to], dst_ref=rows_ref.at[slot], send_sem=send_sems.at[i],
            recv_sem=recv_sems.at[slot], device_id=(to, there), device_id_type=mesh)

    scalars = pltpu.make_async_remote_copy(
        src_ref=mine_ref, dst_ref=next_ref, send_sem=send_sems.at[parts], recv_sem=recv_sems.at[parts],
        device_id=(before, tile), device_id_type=mesh)
    prior = pltpu.make_async_remote_copy(
        src_ref=prior_ref.at[:, own_columns(size, tile)], dst_ref=other_ref.at[:, :size], send_sem=send_sems.at[parts + 1],
        recv_sem=recv_sems.at[parts + 1], device_id=(me, there), device_id_type=mesh)
    scalars.start()
    for i in range(parts - 1, -1, -1):
        rows_copy(i, me).start()
    prior.start()
    scalars.wait()
    last = me == parts - 1
    own, following = mine_ref[...], next_ref[...]
    row = lax.broadcasted_iota(jnp.int32, REG, 0)
    chosen = jnp.where(tile == 0, own, jnp.where(last, 1.0, following))
    numbers_ref[...] = jnp.where(row == 0, chosen, jnp.where(last, 0.0, following))
    for i in range(parts):
        rows_copy(i, me).wait_send()
    for i in range(parts):
        rows_copy(i, lax.rem(me + i, parts)).wait_recv()
    prior.wait()


def exchange(time_diag, rho, first, prior):
    parts = first.shape[0] - 1
    size = prior.shape[0]
    f32 = jnp.float32
    return pl.pallas_call(
        exchange_kernel,
        out_shape=(jax.ShapeDtypeStruct((parts,) + first.shape[1:], f32), jax.ShapeDtypeStruct(prior.shape, f32), jax.ShapeDtypeStruct(REG, f32)),
        in_specs=[pl.BlockSpec(memory_space=pltpu.SMEM)] * 2 + in_vmem(1) + in_hbm(1),
        out_specs=tuple(in_vmem(1) + in_hbm(1) + in_vmem(1)),
        scratch_shapes=[pltpu.VMEM(REG, f32)] * 2 + [pltpu.SemaphoreType.DMA((parts + 2,))] * 2,
        compiler_params=pltpu.CompilerParams(collective_id=0, has_side_effects=True, vmem_limit_bytes=52 << 20),
        cost_estimate=pl.CostEstimate(flops=0, bytes_accessed=4 * size * size, transcendentals=0),
    )(time_diag, rho, first, prior)


def on_device(prior_space, node_gain, time_diag, rho, obs_values, obs_weight, obs_step):
    size = prior_space.shape[0]
    parts = lax.axis_size("tm")
    tile = lax.axis_index("tile")
    first = tile == 0

    def chosen(a, b):
        return jnp.where(first, a, b)

    sent, rest = by_step(obs_values[0], obs_weight[0], obs_step[0, 0], parts)
    rows_other, prior_other, numbers = exchange(time_diag, rho, sent, prior_space)
    rest, rows_other = lax.optimization_barrier((rest, rows_other))
    rest = lax.all_to_all(rest.reshape(parts, -1, size), "tm", split_axis=0, concat_axis=0, tiled=True)

    x, d, log_det, row = first_half(numbers, prior_space, prior_other, rows_other)
    send, own = second_half(x, d, log_det, rest, row, node_gain)
    got = lax.ppermute(send, "tile", [(0, 1), (1, 0)])

    now, following, across = rho[1] * rho[1], numbers[1, 0] * numbers[1, 0], -(rho[0] * rho[1])
    factors = jnp.stack([time_diag[1], chosen(now, following), chosen(following, now), chosen(across, 0.0), chosen(0.0, across)])
    block, coupling, log_det = outputs(factors, prior_space, rest, own, send, got)
    return block[None], coupling[None], log_det[0, :1]


def solution(mesh):
    in_specs = (
        P("tile", None),
        P(),
        P("tm"),
        P("tm"),
        P("tile", "tm", None, None),
        P("tile", "tm", None),
        P("tile", "tm", None),
    )
    out_specs = (P("tm", "tile", None), P("tm", "tile", None), P("tm"))
    return jax.shard_map(
        on_device, mesh=mesh, in_specs=in_specs, out_specs=out_specs, check_vma=False
    )
```

```python
import functools
import jax, jax.numpy as jnp
from jax import lax
from jax.experimental import pallas as pl
from jax.experimental.pallas import tpu as pltpu
from jax.sharding import PartitionSpec as P

REG = (8, 128)
BIG, SMALL = 256, 64


def along(x, j):
    return jnp.broadcast_to(x[:, j:j + 1], REG)


def down(x, i):
    return jnp.take_along_axis(x, jnp.full(REG, i, jnp.int32), axis=0)


def halves(x):
    high = x.astype(jnp.bfloat16)
    return high, (x - high.astype(jnp.float32)).astype(jnp.bfloat16)


def dot_nn(a, b):
    ah, al = halves(a)
    bh, bl = halves(b)
    return jnp.dot(jnp.concatenate([ah, al, ah], 1), jnp.concatenate([bh, bh, bl], 0), preferred_element_type=jnp.float32)


def pair_inverse(a, b, d):
    det = a * d - b * b
    r = 1.0 / det
    return d * r, -(b * r), a * r, det


def inverse_of_four(s):
    a, b, d, det1 = pair_inverse(s[0, 0], s[1, 0], s[1, 1])
    q = [[s[2, 0], s[2, 1]], [s[3, 0], s[3, 1]]]
    m = [[q[i][0] * a + q[i][1] * b, q[i][0] * b + q[i][1] * d] for i in range(2)]
    u = s[2, 2] - (m[0][0] * q[0][0] + m[0][1] * q[0][1])
    v = s[3, 2] - (m[1][0] * q[0][0] + m[1][1] * q[0][1])
    w = s[3, 3] - (m[1][0] * q[1][0] + m[1][1] * q[1][1])
    u, v, w, det2 = pair_inverse(u, v, w)
    low = [[u * m[0][j] + v * m[1][j] for j in range(2)], [v * m[0][j] + w * m[1][j] for j in range(2)]]
    w00 = a + (m[0][0] * low[0][0] + m[1][0] * low[1][0])
    w01 = b + (m[0][0] * low[0][1] + m[1][0] * low[1][1])
    w11 = d + (m[0][1] * low[0][1] + m[1][1] * low[1][1])
    inverse = [[w00, w01, -low[0][0], -low[1][0]],
               [w01, w11, -low[0][1], -low[1][1]],
               [-low[0][0], -low[0][1], u, v],
               [-low[1][0], -low[1][1], v, w]]
    return inverse, det1, det2


def eliminate(tiles, log_det, offset):
    lane = lax.broadcasted_iota(jnp.int32, REG, 1) - offset
    sub = lax.broadcasted_iota(jnp.int32, REG, 0)
    for home in range(len(tiles)):
        p = 8 * home
        cols = [[along(t, offset + p + j) for t in tiles] for j in range(8)]
        c = [cols[j][home] for j in range(8)]
        head, det1, det2 = inverse_of_four({(i, j): down(c[j], i) for j in range(4) for i in range(j, 4)})
        slope = [weighted([head[i][j] for i in range(4)], c[:4]) for j in range(4)]
        rest = [c[j] - weighted([down(c[j], i) for i in range(4)], slope) for j in range(4, 8)]
        foot, det3, det4 = inverse_of_four({(i, j): down(rest[j], i + 4) for j in range(4) for i in range(j, 4)})
        log_det = log_det + ((jnp.log(det1) + jnp.log(det2)) + (jnp.log(det3) + jnp.log(det4)))
        here = (lane >= p) & (lane < p + 8)
        rows = jnp.where(here, jnp.where(lane == p + sub, 1.0, 0.0), tiles[home])
        top = [down(rows, i) for i in range(4)]
        upper = [weighted(head[i], top) for i in range(4)]
        rows = rows - weighted(c[:4], upper)
        low = [down(rows, i) for i in range(4, 8)]
        lower = [weighted(foot[i], low) for i in range(4)]
        upper = [upper[i] - weighted([down(slope[i], j) for j in range(4, 8)], lower) for i in range(4)]
        out = upper + lower
        new = []
        for t, tile in enumerate(tiles):
            if t == home:
                kept = out[0]
                for i in range(1, 8):
                    kept = jnp.where(sub == i, out[i], kept)
            else:
                kept = jnp.where(here, 0.0, tile)
                kept = kept - (weighted([cols[j][t] for j in range(4)], out[:4]) + weighted([cols[j][t] for j in range(4, 8)], out[4:]))
            new.append(kept)
        tiles = new
    return tiles, log_det


def weighted(a, b):
    return (a[0] * b[0] + a[1] * b[1]) + (a[2] * b[2] + a[3] * b[3])


def small_step(s, d_ref, ld_ref):
    half, offset = s // 2, (s % 2) * SMALL
    mine, others = slice(128 * half, 128 * half + 128), slice(128 * (1 - half), 128 * (1 - half) + 128)
    at = slice(SMALL * s, SMALL * s + SMALL)
    tiles = [d_ref[SMALL * s + 8 * t:SMALL * s + 8 * t + 8, mine] for t in range(SMALL // 8)]
    tiles, ld = eliminate(tiles, ld_ref[...], offset)
    ld_ref[...] = ld
    panel = jnp.concatenate(tiles, 0)
    gap = jnp.zeros((SMALL, 128), jnp.float32)

    def inside(rows):
        lane = lax.broadcasted_iota(jnp.int32, (rows, 128), 1)
        return (lane >= offset) & (lane < offset + SMALL)

    def padded(x):
        return jnp.concatenate([x, gap] if offset == 0 else [gap, x], 0)

    across = dot_nn(jnp.where(inside(SMALL), panel, 0.0), padded(d_ref[at, others]))
    d_ref[at, :] = jnp.concatenate([panel, across] if half == 0 else [across, panel], 1)
    left = {}
    for r in [(s + 1 + i) % 4 for i in range(3)]:
        rows = slice(SMALL * r, SMALL * r + SMALL)
        own = d_ref[rows, mine]
        left[r] = jnp.where(inside(SMALL), own, 0.0)
        if offset:
            d_ref[rows, others] -= dot_nn(left[r], padded(across))
            d_ref[rows, mine] = jnp.where(inside(SMALL), 0.0, own) - dot_nn(left[r], padded(panel))
        else:
            d_ref[rows, mine] = jnp.where(inside(SMALL), 0.0, own) - dot_nn(left[r], padded(panel))
            d_ref[rows, others] -= dot_nn(left[r], padded(across))


def dot_nt(a, b):
    k = a.shape[1] // 2
    left = jnp.concatenate([a, a[:, :k]], 1)
    right = jnp.concatenate([b[:, :k], b[:, :k], b[:, k:]], 1)
    return lax.dot_general(left, right, (((1,), (1,)), ((), ())), preferred_element_type=jnp.float32)


def rows_of(i):
    return pl.ds(pl.multiple_of(i * BIG, BIG), BIG)


def split_to(ref, at, x):
    high, low = halves(x)
    ref[at, :BIG] = high
    ref[at, BIG:] = low


def others_of(k, count):
    return [lax.rem(k + 1 + i, count) for i in range(count - 1)]


def gain(i, k, x_ref, c_ref, g_ref, w_ref):
    g = dot_nt(c_ref[rows_of(i), :], w_ref[...])
    split_to(g_ref, rows_of(i), g)
    x_ref[rows_of(i), rows_of(k)] = g


def update(u, v, k, x_ref, c_ref, g_ref):
    low, high = jnp.minimum(u, v), jnp.maximum(u, v)
    r, c = jnp.where(low < k, low, high), jnp.where(low < k, high, low)
    x_ref[rows_of(r), rows_of(c)] -= dot_nt(g_ref[rows_of(r), :], c_ref[rows_of(c), :])


def background(k, count, x_ref, c_ref, g_ref, w_ref):
    others = others_of(k, count)

    def turned(j):
        x_ref[rows_of(k), rows_of(j)] = dot_nt(w_ref[...], c_ref[rows_of(j), :])

    first = [functools.partial(gain, i, k, x_ref, c_ref, g_ref, w_ref) for i in others[1:]]
    first += [functools.partial(turned, j) for j in others]
    pairs = [(a, b) for a in range(count - 1) for b in range(a, count - 1) if b > 0]
    rest = [functools.partial(update, others[a], others[b], k, x_ref, c_ref, g_ref) for a, b in pairs]
    units = first + rest
    share = -(-len(units) // 4)
    return [units[i * share:(i + 1) * share] for i in range(4)]


def boundary(k, x_ref, d_ref, c_ref, g_ref, w_ref):
    count = x_ref.shape[0] // BIG
    q = k + 1
    w = d_ref[...]
    split_to(w_ref, slice(None), w)
    x_ref[rows_of(k), rows_of(k)] = -w
    split_to(c_ref, rows_of(q), x_ref[rows_of(q), rows_of(k)])
    for r in range(0, BIG, SMALL):
        rows = pl.ds(pl.multiple_of(q * BIG + r, SMALL), SMALL)
        split_to(g_ref, rows, dot_nt(c_ref[rows, :], w_ref[...]))
        d_ref[r:r + SMALL, :] = x_ref[rows, rows_of(q)] - dot_nt(g_ref[rows, :], c_ref[rows_of(q), :])
    for i in others_of(k, count)[1:]:
        split_to(c_ref, rows_of(i), x_ref[rows_of(i), rows_of(k)])


def eliminate_blocks(start, stop, x_ref, ld_ref, d_ref, c_ref, g_ref, w_ref):
    count = x_ref.shape[0] // BIG

    def body(q, _):
        boundary(q - 1, x_ref, d_ref, c_ref, g_ref, w_ref)
        work = background(q - 1, count, x_ref, c_ref, g_ref, w_ref)
        for s in range(BIG // SMALL):
            small_step(s, d_ref, ld_ref)
            for unit in work[s]:
                unit()
        return 0

    lax.fori_loop(start, stop, body, 0)


def turned_halves(ref, u):
    split_at = u.shape[0]
    high, low = halves(u.T)
    ref[:, :split_at] = high
    ref[:, split_at:] = low


def blocks_of(size):
    return [slice(i, i + BIG) for i in range(0, size, BIG)]


def stacked(ref, part):
    depth = ref.shape[1] // 2 if part is not None else ref.shape[1]
    at = slice((part or 0) * depth, (part or 0) * depth + depth)
    return jnp.concatenate([ref[m, at, :] for m in range(ref.shape[0])], 0)


def own_columns(size, tile):
    return pl.ds(pl.multiple_of(tile * size, 128), size)


def column_of(row):
    here = lax.broadcasted_iota(jnp.int32, (128, 128), 0) == lax.broadcasted_iota(jnp.int32, (128, 128), 1)
    parts = [jnp.sum(jnp.where(here, row[:, i:i + 128], 0.0), 1, keepdims=True) for i in range(0, row.shape[1], 128)]
    return jnp.concatenate(parts, 0)


def split_scaled(ref, turned, scale):
    split_at = turned.shape[1]
    high, low = halves(turned * scale)
    ref[:, :split_at] = high
    ref[:, split_at:] = low


def first_kernel(numbers_ref, prior_in_ref, other_in_ref, rows_ref,
                 x_ref, d_ref, ld_ref, row_ref, c_ref, g_ref, w_ref, u_ref, col_ref, other_ref, prior_ref, in_sems):
    size = other_ref.shape[0]
    tile = lax.axis_index("tile")
    own_at, other_at = tile * size, (1 - tile) * size
    fetches = [pltpu.make_async_copy(other_in_ref.at[:, :size], other_ref, in_sems.at[0]),
               pltpu.make_async_copy(prior_in_ref, prior_ref, in_sems.at[1])]
    for fetch in fetches:
        fetch.start()
    weight_row, weight = numbers_ref[0:1, :], numbers_ref[0:1, 0:1]
    here = lax.broadcasted_iota(jnp.int32, (128, 128), 0) == lax.broadcasted_iota(jnp.int32, (128, 128), 1)

    def scale_at(i, square):
        row_ref[:, i:i + 128] = lax.rsqrt(weight_row * jnp.sum(jnp.where(here, square, 0.0), 0, keepdims=True))

    turned = stacked(rows_ref, None).T
    fetches[0].wait()
    for i in range(0, size, 128):
        scale_at(i, other_ref[i:i + 128, i:i + 128])
    col_ref[:size, :] = column_of(row_ref[:, :size])
    split_scaled(u_ref, turned, col_ref[:size, :])
    blocks = blocks_of(size)

    def corner(at, to):
        return other_ref[at, to] * (col_ref[at, :] * weight) * row_ref[:, to] + dot_nt(u_ref[at, :], u_ref[to, :])

    def build_other(at, to):
        x_ref[at, to] = corner(at, to)

    def build_low(at, to, base, start):
        low, far = slice(size + at.start, size + at.stop), slice(base + to.start, base + to.stop)
        cols = pl.ds(pl.multiple_of(start + to.start, 128), BIG)
        x_ref[low, far] = prior_ref[at, cols] * (col_ref[low, :] * weight) * row_ref[:, far]

    ld_ref[...] = jnp.zeros_like(ld_ref)
    d_ref[...] = corner(blocks[0], blocks[0])
    fetches[1].wait()
    for i in range(0, size, 128):
        scale_at(size + i, prior_ref[i:i + 128, pl.ds(pl.multiple_of(own_at + i, 128), 128)])
    col_ref[size:, :] = column_of(row_ref[:, size:])
    units = []
    for i, at in enumerate(blocks):
        units += [functools.partial(build_other, at, to) for j, to in enumerate(blocks) if 0 < i and j <= i]
        units += [functools.partial(build_low, at, to, 0, other_at) for to in blocks]
        units += [functools.partial(build_low, at, to, size, own_at) for j, to in enumerate(blocks) if j <= i]
    steps = BIG // SMALL
    for s in range(steps):
        small_step(s, d_ref, ld_ref)
        for unit in units[s::steps]:
            unit()
    eliminate_blocks(1, size // BIG, x_ref, ld_ref, d_ref, c_ref, g_ref, w_ref)


def upper_place(i, j, count):
    return i * count - i * (i - 1) // 2 + j - i


def second_kernel(x_in_ref, d_in_ref, ld_in_ref, rows_ref, row_ref, gain_ref,
                  send_out_ref, own_out_ref, x_ref, d_ref, c_ref, g_ref, w_ref, u_ref, left_ref, left_col_ref, ld_ref,
                  send_ref, own_ref, in_sem, out_sems):
    n = x_ref.shape[0]
    size = n // 2
    count = n // BIG
    half = size // BIG
    fetch = pltpu.make_async_copy(x_in_ref, x_ref, in_sem)
    fetch.start()
    d_ref[...] = d_in_ref[...]
    ld_ref[...] = ld_in_ref[...]
    turned_halves(u_ref, stacked(rows_ref, 0) * row_ref[:, size:])
    tile = lax.axis_index("tile")
    left_ref[:, :size] = row_ref[:, :size] * gain_ref[:, own_columns(size, 1 - tile)]
    left_ref[:, size:] = row_ref[:, size:] * gain_ref[:, own_columns(size, tile)]
    left_col_ref[...] = column_of(left_ref[...])
    fetch.wait()
    for i, at in enumerate(blocks_of(size)):
        for j, to in enumerate(blocks_of(size)):
            if j <= i:
                x_ref[size + at.start:size + at.stop, size + to.start:size + to.stop] += dot_nt(u_ref[at, :], u_ref[to, :])
    eliminate_blocks(half, count, x_ref, ld_ref, d_ref, c_ref, g_ref, w_ref)
    k = count - 1
    w = d_ref[...]
    split_to(w_ref, slice(None), w)

    def finish(a, b, value):
        rows, cols = slice(a * BIG, a * BIG + BIG), slice(b * BIG, b * BIG + BIG)
        value = -value * left_col_ref[rows, :] * left_ref[:, cols]
        if b < half:
            place = half * half + upper_place(a, b, half)
        else:
            place = a * half + b - half if a < half else upper_place(a - half, b - half, half)
        ref = send_ref if a < half else own_ref
        ref[place * BIG:place * BIG + BIG, :] = value

    total = ld_ref[...] - 2.0 * jnp.sum(jnp.log(row_ref[...]))
    send_ref[send_ref.shape[0] - REG[0]:, :] = jnp.concatenate([total] * (BIG // REG[1]), 1)
    finish(k, k, -w)
    for i in range(k):
        at = slice(i * BIG, i * BIG + BIG)
        c = x_ref[at, k * BIG:n]
        split_to(c_ref, at, c)
        g = dot_nt(c_ref[at, :], w_ref[...])
        split_to(g_ref, at, g)
        finish(i, k, g)
    for a in range(k):
        at = slice(a * BIG, a * BIG + BIG)
        for b in range(a, k):
            to = slice(b * BIG, b * BIG + BIG)
            finish(a, b, x_ref[at, to] - dot_nt(g_ref[at, :], c_ref[to, :]))
        if a == half - 1:
            send = pltpu.make_async_copy(send_ref, send_out_ref, out_sems.at[0])
            send.start()
    own = pltpu.make_async_copy(own_ref, own_out_ref.at[:own_ref.shape[0]], out_sems.at[1])
    own.start()
    send.wait()
    own.wait()


def states(n, rows):
    return [
        pltpu.VMEM((n, 2 * BIG), jnp.bfloat16),
        pltpu.VMEM((n, 2 * BIG), jnp.bfloat16),
        pltpu.VMEM((BIG, 2 * BIG), jnp.bfloat16),
        pltpu.VMEM((n // 2, 2 * rows), jnp.bfloat16),
    ]


def in_vmem(count):
    return [pl.BlockSpec(memory_space=pltpu.VMEM)] * count


def in_hbm(count):
    return [pl.BlockSpec(memory_space=pltpu.HBM)] * count


def first_half(numbers, prior, other, rows):
    size, n = prior.shape
    f32 = jnp.float32
    return pl.pallas_call(
        first_kernel,
        out_shape=(jax.ShapeDtypeStruct((n, n), f32), jax.ShapeDtypeStruct((BIG, BIG), f32), jax.ShapeDtypeStruct(REG, f32),
                   jax.ShapeDtypeStruct((1, n), f32)),
        in_specs=in_vmem(1) + in_hbm(2) + in_vmem(1),
        out_specs=tuple(in_vmem(4)),
        scratch_shapes=states(n, rows.shape[0] * rows.shape[1]) + [pltpu.VMEM((n, 1), f32), pltpu.VMEM((size, size), f32), pltpu.VMEM((size, n), f32), pltpu.SemaphoreType.DMA((2,))],
        compiler_params=pltpu.CompilerParams(vmem_limit_bytes=52 << 20),
        cost_estimate=pl.CostEstimate(flops=12 * n**3, bytes_accessed=8 * n * n, transcendentals=0),
    )(numbers, prior, other, rows)


def second_half(x, d, log_det, rows, row, gain):
    n = x.shape[0]
    size = n // 2
    f32 = jnp.float32
    half = size // BIG
    upper = half * (half + 1) // 2 * BIG
    send, own = (half * size + upper + REG[0], BIG), (upper, BIG)
    return pl.pallas_call(
        second_kernel,
        out_shape=(jax.ShapeDtypeStruct(send, f32),) * 2,
        in_specs=in_hbm(1) + in_vmem(5),
        out_specs=tuple(in_hbm(2)),
        scratch_shapes=[pltpu.VMEM((n, n), f32), pltpu.VMEM((BIG, BIG), f32)] + states(n, rows.shape[0] * rows.shape[1] // 2)
        + [pltpu.VMEM((1, n), f32), pltpu.VMEM((n, 1), f32), pltpu.VMEM(REG, f32), pltpu.VMEM(send, f32),
           pltpu.VMEM(own, f32), pltpu.SemaphoreType.DMA, pltpu.SemaphoreType.DMA((2,))],
        compiler_params=pltpu.CompilerParams(vmem_limit_bytes=52 << 20),
        cost_estimate=pl.CostEstimate(flops=12 * n**3, bytes_accessed=8 * n * n, transcendentals=0),
    )(x, d, log_det, rows, row, gain[None, :])


def last_kernel(numbers_ref, prior_in_ref, rows_ref, own_in_ref, sent_in_ref, got_in_ref,
                block_ref, coupling_ref, log_ref, prior_ref, own_ref, sent_ref, got_ref, block_buf, coupling_buf, u_ref, in_sems, sems):
    size, n = prior_ref.shape
    tile = lax.axis_index("tile")
    own_at = tile * size
    cross_at = size - own_at
    blocks = blocks_of(size)
    half = len(blocks)
    corner = half * size
    fetches = [pltpu.make_async_copy(own_in_ref.at[:own_ref.shape[0]], own_ref, in_sems.at[0]),
               pltpu.make_async_copy(sent_in_ref.at[:corner], sent_ref.at[:corner], in_sems.at[1]),
               pltpu.make_async_copy(got_in_ref.at[corner:], got_ref.at[corner:], in_sems.at[2]),
               pltpu.make_async_copy(sent_in_ref.at[sent_ref.shape[0] - REG[0]:], sent_ref.at[sent_ref.shape[0] - REG[0]:], in_sems.at[3])]
    for i, at in enumerate(blocks):
        part = slice(i * size, i * size + size)
        fetches.append(pltpu.make_async_copy(prior_in_ref.at[at], prior_ref.at[at], in_sems.at[4 + 2 * i]))
        fetches.append(pltpu.make_async_copy(got_in_ref.at[part], got_ref.at[part], in_sems.at[5 + 2 * i]))
    for fetch in fetches:
        fetch.start()

    def block(ref, place):
        return ref[place * BIG:place * BIG + BIG, :]

    def mirrored(ref, first, i, j):
        return block(ref, first + upper_place(i, j, half)) if i <= j else block(ref, first + upper_place(j, i, half)).T

    weight, have_block, got_block, have_coupling, got_coupling = [numbers_ref[i] for i in range(5)]
    turned_halves(u_ref, stacked(rows_ref, 1))
    copies = []
    for i, at in enumerate(blocks):
        for fetch in (fetches[:6] if i == 0 else fetches[4 + 2 * i:6 + 2 * i]):
            fetch.wait()
        for j, to in enumerate(blocks):
            for which in range(2):
                if which == 0:
                    have = mirrored(own_ref, 0, i, j)
                    got = mirrored(got_ref, half * half, i, j)
                    cols = pl.ds(pl.multiple_of(own_at + j * BIG, BIG), BIG)
                else:
                    have = block(sent_ref, j * half + i).T
                    got = block(got_ref, i * half + j)
                    cols = pl.ds(pl.multiple_of(cross_at + j * BIG, BIG), BIG)
                base = weight * prior_ref[at, cols]
                if which == 0:
                    base = base + dot_nt(u_ref[at, :], u_ref[to, :])
                block_buf[at, cols] = base - (have_block * have + got_block * got)
                coupling_buf[at, cols] = have_coupling * have + got_coupling * got
        for o, (buf, ref) in enumerate([(block_buf, block_ref), (coupling_buf, coupling_ref)]):
            copy = pltpu.make_async_copy(buf.at[at], ref.at[at], sems.at[2 * i + o])
            copy.start()
            copies.append(copy)
    foot = slice(got_ref.shape[0] - REG[0], got_ref.shape[0])
    log_ref[...] = jnp.where(tile == 0, sent_ref[foot, :REG[1]], got_ref[foot, :REG[1]]) / n
    for copy in copies:
        copy.wait()


def outputs(numbers, prior, rows, own, send, got):
    size, n = prior.shape
    f32 = jnp.float32
    count = size // BIG
    return pl.pallas_call(
        last_kernel,
        out_shape=(jax.ShapeDtypeStruct((size, n), f32),) * 2 + (jax.ShapeDtypeStruct(REG, f32),),
        in_specs=[pl.BlockSpec(memory_space=pltpu.SMEM)] + in_hbm(1) + in_vmem(1) + in_hbm(3),
        out_specs=tuple(in_hbm(2) + in_vmem(1)),
        scratch_shapes=[pltpu.VMEM((size, n), f32), pltpu.VMEM((count * (count + 1) // 2 * BIG, BIG), f32), pltpu.VMEM(send.shape, f32), pltpu.VMEM(got.shape, f32)] + [pltpu.VMEM((size, n), f32)] * 2
        + [pltpu.VMEM((size, rows.shape[0] * rows.shape[1]), jnp.bfloat16), pltpu.SemaphoreType.DMA((2 * count + 4,)),
           pltpu.SemaphoreType.DMA((2 * count,))],
        compiler_params=pltpu.CompilerParams(vmem_limit_bytes=52 << 20),
        cost_estimate=pl.CostEstimate(flops=6 * size * size * n, bytes_accessed=20 * size * n, transcendentals=0),
    )(numbers, prior, rows, own, send, got)


def order_kernel(step_ref, value_ref, weight_ref, first_ref, rest_ref):
    parts = first_ref.shape[0] - 1
    tile = lax.axis_index("tile")
    root = jnp.sqrt(weight_ref[...]).T
    for k in range(value_ref.shape[0]):
        step = step_ref[k]
        part, odd = lax.shift_right_logical(step, 1), (step & 1) == 1
        rows = value_ref[k] * root[:, k:k + 1]
        before = jnp.where(part == 0, parts - 1, part - 1)
        at_zero, at_one = part, before
        first_ref[jnp.where(odd, parts, jnp.where(tile == 0, at_one, at_zero))] = rows
        rest_ref[2 * jnp.where(odd | (tile == 0), at_zero, at_one) + (step & 1)] = rows


def by_step(values, weights, steps, parts):
    depth, size = values.shape[1:]
    return pl.pallas_call(
        order_kernel,
        out_shape=(jax.ShapeDtypeStruct((parts + 1, depth, size), jnp.float32), jax.ShapeDtypeStruct((2 * parts, depth, size), jnp.float32)),
        in_specs=[
            pl.BlockSpec(memory_space=pltpu.SMEM),
            pl.BlockSpec(memory_space=pltpu.VMEM),
            pl.BlockSpec(memory_space=pltpu.VMEM),
        ],
        out_specs=tuple(in_vmem(2)),
        compiler_params=pltpu.CompilerParams(vmem_limit_bytes=40 << 20),
    )(steps, values, weights)


def exchange_kernel(time_ref, rho_ref, first_ref, prior_ref, rows_ref, other_ref, numbers_ref, mine_ref, next_ref, send_sems, recv_sems):
    parts = rows_ref.shape[0]
    size = prior_ref.shape[0]
    me, tile = lax.axis_index("tm"), lax.axis_index("tile")
    there = 1 - tile
    after, before = lax.rem(me + 1, parts), lax.rem(me + parts - 1, parts)
    mesh = pl.DeviceIdType.MESH
    barrier = pltpu.get_barrier_semaphore()
    for i in range(parts):
        pl.semaphore_signal(barrier, inc=1, device_id=(lax.rem(me + i, parts), there), device_id_type=mesh)
    pl.semaphore_signal(barrier, inc=1, device_id=(after, tile), device_id_type=mesh)
    mine_ref[0:1, :] = jnp.full((1, REG[1]), time_ref[0], jnp.float32)
    mine_ref[1:2, :] = jnp.full((1, REG[1]), rho_ref[0], jnp.float32)
    mine_ref[2:, :] = jnp.zeros((REG[0] - 2, REG[1]), jnp.float32)
    pl.semaphore_wait(barrier, parts + 1)

    def rows_copy(i, slot):
        to = lax.rem(me + i, parts)
        return pltpu.make_async_remote_copy(
            src_ref=first_ref.at[to], dst_ref=rows_ref.at[slot], send_sem=send_sems.at[i],
            recv_sem=recv_sems.at[slot], device_id=(to, there), device_id_type=mesh)

    scalars = pltpu.make_async_remote_copy(
        src_ref=mine_ref, dst_ref=next_ref, send_sem=send_sems.at[parts], recv_sem=recv_sems.at[parts],
        device_id=(before, tile), device_id_type=mesh)
    prior = pltpu.make_async_remote_copy(
        src_ref=prior_ref.at[:, own_columns(size, tile)], dst_ref=other_ref.at[:, :size], send_sem=send_sems.at[parts + 1],
        recv_sem=recv_sems.at[parts + 1], device_id=(me, there), device_id_type=mesh)
    scalars.start()
    for i in range(parts - 1, -1, -1):
        rows_copy(i, me).start()
    prior.start()
    scalars.wait()
    last = me == parts - 1
    own, following = mine_ref[...], next_ref[...]
    row = lax.broadcasted_iota(jnp.int32, REG, 0)
    chosen = jnp.where(tile == 0, own, jnp.where(last, 1.0, following))
    numbers_ref[...] = jnp.where(row == 0, chosen, jnp.where(last, 0.0, following))
    for i in range(parts):
        rows_copy(i, me).wait_send()
    for i in range(parts):
        rows_copy(i, lax.rem(me + i, parts)).wait_recv()
    prior.wait()


def exchange(time_diag, rho, first, prior):
    parts = first.shape[0] - 1
    size = prior.shape[0]
    f32 = jnp.float32
    return pl.pallas_call(
        exchange_kernel,
        out_shape=(jax.ShapeDtypeStruct((parts,) + first.shape[1:], f32), jax.ShapeDtypeStruct(prior.shape, f32), jax.ShapeDtypeStruct(REG, f32)),
        in_specs=[pl.BlockSpec(memory_space=pltpu.SMEM)] * 2 + in_vmem(1) + in_hbm(1),
        out_specs=tuple(in_vmem(1) + in_hbm(1) + in_vmem(1)),
        scratch_shapes=[pltpu.VMEM(REG, f32)] * 2 + [pltpu.SemaphoreType.DMA((parts + 2,))] * 2,
        compiler_params=pltpu.CompilerParams(collective_id=0, has_side_effects=True, vmem_limit_bytes=52 << 20),
        cost_estimate=pl.CostEstimate(flops=0, bytes_accessed=4 * size * size, transcendentals=0),
    )(time_diag, rho, first, prior)


def on_device(prior_space, node_gain, time_diag, rho, obs_values, obs_weight, obs_step):
    size = prior_space.shape[0]
    parts = lax.axis_size("tm")
    tile = lax.axis_index("tile")
    first = tile == 0

    def chosen(a, b):
        return jnp.where(first, a, b)

    sent, rest = by_step(obs_values[0], obs_weight[0], obs_step[0, 0], parts)
    rows_other, prior_other, numbers = exchange(time_diag, rho, sent, prior_space)
    rest, rows_other = lax.optimization_barrier((rest, rows_other))
    rest = lax.all_to_all(rest.reshape(parts, -1, size), "tm", split_axis=0, concat_axis=0, tiled=True)

    x, d, log_det, row = first_half(numbers, prior_space, prior_other, rows_other)
    send, own = second_half(x, d, log_det, rest, row, node_gain)
    got = lax.ppermute(send, "tile", [(0, 1), (1, 0)])

    now, following, across = rho[1] * rho[1], numbers[1, 0] * numbers[1, 0], -(rho[0] * rho[1])
    factors = jnp.stack([time_diag[1], chosen(now, following), chosen(following, now), chosen(across, 0.0), chosen(0.0, across)])
    block, coupling, log_det = outputs(factors, prior_space, rest, own, send, got)
    return block[None], coupling[None], log_det[0, :1]


def solution(mesh):
    in_specs = (
        P("tile", None),
        P(),
        P("tm"),
        P("tm"),
        P("tile", "tm", None, None),
        P("tile", "tm", None),
        P("tile", "tm", None),
    )
    out_specs = (P("tm", "tile", None), P("tm", "tile", None), P("tm"))
    return jax.shard_map(
        on_device, mesh=mesh, in_specs=in_specs, out_specs=out_specs, check_vma=False
    )
```
